256 devices in a mesh: vec: 16 (over z, y_lo), grid: 16 (over x, y_hi, core).
Axes of the slice: x: 4, y: 4 (y_hi: 2, y_lo: 2; y = y_hi * 2 + y_lo), z: 8, core: 2. Of those that a mesh axis runs over, the one named last changes fastest.
Arguments:
- fitting_vectors: float32 [256, 32, 1024], P('vec', 'grid'), may hold values from -6 to 6
Outputs:
- coulomb_blocks: float32 [256, 9, 16], P(('vec', 'grid'))
The draws below stay inside these ranges and needn't reach their ends.
All inputs are finite; a program needn't handle non-finite values.
Results may differ from the reference program's by a relative error of at most 0.00005.
Values sent between devices are 32-bit elements; how exact they have to be, the bound alone decides.
A program may use at most 64 MiB of HBM per device.

```python
import math
import jax
import jax.numpy as jnp
from jax import lax

N = 32
PAD = 64
GROUPS = 16
VG = 16
VECTORS = 256
SHIFTS = 9


def level_of(rng, dims, split, smallest, top_value):
    def one(dim, parts):
        heights = jax.random.uniform(jax.random.fold_in(jax.random.fold_in(rng, 6), dim), (parts,), jnp.float32, smallest / len(split), top_value / len(split))
        return jnp.repeat(jnp.exp(heights), dims[dim] // parts).reshape((-1,) + (1,) * (len(dims) - dim - 1))

    factor_of = one(*split[0])
    for cut in split[1:]:
        factor_of = factor_of * one(*cut)
    return factor_of


def gaussian(stream_key, dims, deviation, limit, split=(), held_as=jnp.bfloat16):
    drawn = jax.random.normal(stream_key, dims, jnp.float32) * deviation
    if len(split) > 0:
        drawn = level_of(stream_key, dims, split, -0.22, 0.18) * drawn
    return jnp.clip(drawn, min=-limit, max=limit).astype(held_as)


def setup_inputs(seed: int = 0) -> dict:
    key_list = jax.random.split(jax.random.key(seed), 2)
    fitting_vectors = gaussian(key_list[0], (VECTORS, N, N * N), 1.0, 6.0, ((0, 16), (1, 16)), jnp.float32)
    return {"fitting_vectors": fitting_vectors}


def kernel_half(size, padded):
    full = jnp.arange(padded, dtype=jnp.int32)
    signed = jnp.where(full < padded // 2, full, full - padded).astype(jnp.float32)
    last = jnp.arange(padded // 2 + 1, dtype=jnp.int32).astype(jnp.float32)
    total_sq = (signed * signed)[:, None, None] + (signed * signed)[None, :, None] + (last * last)[None, None, :]
    wave_sq = total_sq * (2.0 * math.pi / padded) ** 2
    safe_sq = jnp.where(total_sq > 0, wave_sq, 1.0)
    half_arg = 0.5 * jnp.sqrt(safe_sq) * size
    values = 8.0 * math.pi * jnp.sin(half_arg) ** 2 / safe_sq
    anchor = 2.0 * math.pi * size * size
    return jnp.where(total_sq > 0, values, anchor)

def reference(fitting_vectors):
    kernel = kernel_half(N, PAD)

    def potential_of(field):
        cube = field.reshape(N, N, N)
        spectrum = jnp.fft.rfftn(cube, s=(PAD, PAD, PAD))
        result = jnp.fft.irfftn(spectrum * kernel, s=(PAD, PAD, PAD))[:N, :N, :N]
        return result.reshape(N, N * N)
    potentials = lax.map(potential_of, fitting_vectors)
    flat_vectors = fitting_vectors.reshape(VECTORS, -1)
    flat_potentials = potentials.reshape(VECTORS, -1)
    gram = jnp.dot(flat_vectors, flat_potentials.T, precision=lax.Precision.HIGHEST, preferred_element_type=jnp.float32) / float(N ** 3)
    row_index = jnp.arange(VECTORS, dtype=jnp.int32)[:, None, None]
    offset_index = jnp.arange(SHIFTS, dtype=jnp.int32)[None, :, None]
    within_index = jnp.arange(VG, dtype=jnp.int32)[None, None, :]
    column_index = (row_index // VG + offset_index) % GROUPS * VG + within_index
    return gram[row_index, column_index]
```

```python
import functools
import math

import jax
import jax.numpy as jnp
import numpy as np
from jax import lax
from jax.experimental import pallas as pl
from jax.experimental.pallas import tpu as pltpu
from jax.sharding import PartitionSpec as P

N = 32
PAD = 2 * N
F32 = jnp.float32
BF16 = jnp.bfloat16
MESH = pl.DeviceIdType.MESH
REACH = 4


def tables():
    pos = np.arange(N) - (N - 1) / 2.0
    freqs = np.concatenate([np.arange(N), np.arange(1, N + 1)])
    phase = 2.0 * np.pi * freqs[:, None] * pos[None, :] / PAD
    trig = np.where(np.arange(PAD)[:, None] < N, np.cos(phase), np.sin(phase))
    weight = np.where((freqs == 0) | (freqs == N), 1.0, 2.0)
    f = freqs.astype(np.float64)
    total = f[:, None, None] ** 2 + f[None, :, None] ** 2 + f[None, None, :] ** 2
    g2 = total * (2.0 * np.pi / PAD) ** 2
    safe = np.where(total > 0, g2, 1.0)
    kernel = 8.0 * np.pi * np.sin(np.sqrt(safe) * (N / 2)) ** 2 / safe
    kernel = np.where(total > 0, kernel, 2.0 * np.pi * N * N)
    kernel = kernel * weight[:, None, None] * weight[None, :, None] * weight[None, None, :]
    kernel = kernel / float(PAD) ** 3 / float(N) ** 3
    return trig, kernel


def split_np(a):
    hi = a.astype(np.float32).astype(BF16)
    lo = (a - hi.astype(np.float64)).astype(np.float32).astype(BF16)
    return hi, lo


def constants():
    trig, kernel = tables()
    row = np.arange(N)
    y_of_row = 4 * (row % 8) + row // 8
    ty = trig[:, y_of_row]
    hi, lo = split_np(ty)
    ly = np.concatenate([hi, hi, lo], axis=1)
    hi, lo = split_np(ty.T)
    lyi = np.concatenate([hi, hi, lo], axis=1)
    hi, lo = split_np(np.kron(np.eye(8), trig.T))
    bz = np.stack([hi, lo])
    hi, lo = split_np(np.kron(np.eye(4), trig))
    bzi = np.concatenate([hi, lo], axis=1)
    kt = kernel.reshape(8, 8, PAD, PAD).transpose(0, 2, 1, 3).reshape(8 * PAD, 8 * PAD)
    return ly, lyi, bz, bzi, kt.astype(np.float32), trig


def split(x):
    hi = x.astype(BF16)
    lo = (x - hi.astype(F32)).astype(BF16)
    return hi, lo


def dot(a, b):
    return jnp.dot(a, b, preferred_element_type=F32)


def dot_nt(a, b):
    return lax.dot_general(a, b, (((1,), (1,)), ((), ())), preferred_element_type=F32)


def combine(matrix, values):
    out = []
    for weights in matrix:
        acc = None
        for w, v in zip(weights, values):
            term = v * np.float32(w)
            acc = term if acc is None else acc + term
        out.append(acc)
    return out


def swap_chunks(tiles, odd1, odd2):
    t0, t1, t2, t3 = tiles

    def pair(a, b, mask, up, down):
        return (
            jnp.where(mask, pltpu.roll(b, up, 1), a),
            jnp.where(mask, b, pltpu.roll(a, down, 1)),
        )

    a0, a1 = pair(t0, t1, odd1, 32, 96)
    a2, a3 = pair(t2, t3, odd1, 32, 96)
    b0, b2 = pair(a0, a2, odd2, 64, 64)
    b1, b3 = pair(a1, a3, odd2, 64, 64)
    return b0, b1, b2, b3


def body_kernel(
    trig,
    v_in, ly_in, lyi_in, bz_in, bzi_in, kt_in,
    out_ref,
    u, pbuf, pl_in, vl, ly, lyi, bz, bzi, kt,
    m1, m2h, m2l, m3h, m3l, m4, m5, vh, vlo, sb, rl,
    c_sem, a1_send, a1_recv, v_send, v_recv, v_loc, a2_send, a2_recv, a2_loc, r_send, r_recv, r_loc,
):
    g = lax.axis_index("vec")
    r = lax.axis_index("grid")
    half = lax.rem(g, 2)
    sib = g + 1 - 2 * half
    down = lax.rem(g + 14, 16)
    down_sib = lax.rem(sib + 14, 16)
    up = lax.rem(g + 2, 16)
    up_sib = lax.rem(sib + 2, 16)
    base = g - half
    me = half * 16 + r

    consts = [
        pltpu.make_async_copy(a, b, c_sem.at[i])
        for i, (a, b) in enumerate([(ly_in, ly), (lyi_in, lyi), (bz_in, bz), (bzi_in, bzi), (kt_in, kt)])
    ]
    for c in consts:
        c.start()
    own = pltpu.make_async_copy(
        v_in.at[:, pl.ds(8 * half, 8), :], vl.at[pl.ds(16 * half, 16)], v_loc
    )
    own.start()

    barrier = pltpu.get_barrier_semaphore()

    def greet(i, _):
        p = lax.rem(me + i, 32)
        pl.semaphore_signal(
            barrier, inc=1, device_id=(base + p // 16, lax.rem(p, 16)), device_id_type=MESH
        )
        return 0

    lax.fori_loop(1, 32, greet, 0)
    for other in (down, down_sib, up, up_sib):
        pl.semaphore_signal(barrier, inc=1, device_id=(other, r), device_id_type=MESH)
    pl.semaphore_wait(barrier, 35)

    def send_slab(m, _):
        pltpu.make_async_remote_copy(
            v_in.at[m], u.at[pl.ds(16 * r, 16)], a1_send, a1_recv,
            device_id=(sib, m), device_id_type=MESH,
        ).start()
        return 0

    lax.fori_loop(0, 16, send_slab, 0)

    def move(src, d, part, sem, target):
        return pltpu.make_async_remote_copy(
            src, vl.at[pl.ds(32 * d + 16 * part, 16)], v_send.at[sem], v_recv.at[sem],
            device_id=(target, r), device_id_type=MESH,
        )

    mine = v_in.at[:, pl.ds(8 * half, 8), :]
    other = v_in.at[:, pl.ds(8 * (1 - half), 8), :]
    first = [
        move(mine, 1, half, 1, down),
        move(other, 1, half, 2, down_sib),
        move(other, 0, half, 0, sib),
    ]
    for c in first:
        c.start()

    def wait_part(d, part, sem):
        ref = vl.at[pl.ds(32 * d + 16 * part, 16)]
        pltpu.make_async_copy(ref, ref, v_recv.at[sem]).wait()

    def relay(d):
        for k in range(2):
            part = half if k == 0 else 1 - half
            wait_part(d, part, 2 * d - 1 + k)
            if d < REACH:
                ref = vl.at[pl.ds(32 * d + 16 * part, 16)]
                move(ref, d + 1, part, 2 * d + 1 + k, down).start()

    relay(1)
    for c in consts:
        c.wait()
    pltpu.make_async_copy(u, u, a1_recv).wait()

    lane = lax.broadcasted_iota(jnp.int32, (8, 128), 1) // 32
    odd1 = lane % 2 == 1
    odd2 = lane >= 2

    def plane(x):
        return u[pl.ds(16 * (x // 2) + x % 2, 8, stride=2), :]

    low = [plane(15 - n) for n in range(16)]
    high = [plane(16 + n) for n in range(16)]
    for part in range(2):
        if part == 0:
            vals = [a + b for a, b in zip(high, low)]
        else:
            vals = [a - b for a, b in zip(high, low)]
        for a in range(8):
            q = 32 * part + 4 * a
            tiles = combine(trig[q:q + 4, 16:32], vals)
            tile = jnp.concatenate(swap_chunks(tiles, odd1, odd2), axis=0)
            hi, lo = split(tile)
            cols = pl.ds((8 * part + a) * 128, 128)
            m1[0:32, cols] = hi
            m1[32:64, cols] = lo
            m1[64:96, cols] = hi

    for n in range(8):
        hi, lo = split(dot(ly[...], m1[:, 256 * n:256 * n + 256]))
        m2h[64 * n:64 * n + 64, :] = hi
        m2l[64 * n:64 * n + 64, :] = lo

    for n in range(4):
        rows = slice(128 * n, 128 * n + 128)
        t = dot(m2h[rows, :], bz[0]) + dot(m2l[rows, :], bz[0]) + dot(m2h[rows, :], bz[1])
        hi, lo = split(t * kt[rows, :])
        m3h[rows, :] = hi
        m3l[rows, :] = lo

    relay(2)

    for n in range(8):
        rows = slice(64 * n, 64 * n + 64)
        for h in range(2):
            cols = slice(256 * h, 256 * h + 256)
            w = dot(m3h[rows, cols], bzi[...])
            t = w[:, 0:128] + w[:, 128:256] + dot(m3l[rows, cols], bzi[:, 0:128])
            hi, lo = split(t)
            out = pl.ds((2 * n + h) * 128, 128)
            m4[0:64, out] = hi
            m4[64:128, out] = lo
            m4[128:192, out] = hi

    for n in range(8):
        cols = slice(256 * n, 256 * n + 256)
        m5[:, cols] = dot(lyi[...], m4[:, cols])

    sums = []
    for part in range(2):
        vals = []
        for a in range(8):
            cols = slice((8 * part + a) * 128, (8 * part + a) * 128 + 128)
            vals += swap_chunks([m5[8 * j:8 * j + 8, cols] for j in range(4)], odd1, odd2)
        sums.append(combine(trig[32 * part:32 * part + 32, 16:32].T, vals))
    for n in range(16):
        for x, val in ((16 + n, sums[0][n] + sums[1][n]), (15 - n, sums[0][n] - sums[1][n])):
            pbuf[pl.ds(16 * (x // 2) + x % 2, 8, stride=2), :] = val

    slot = (1 - half) * 16 + r

    def send_potential(i, _):
        p = lax.rem(me + i, 32)
        rows = pl.multiple_of(16 * lax.rem(p, 16) + 8 * (p // 16), 8)
        pltpu.make_async_remote_copy(
            pbuf.at[pl.ds(rows, 8)], pl_in.at[slot], a2_send, a2_recv,
            device_id=(base + p // 16, lax.rem(p, 16)), device_id_type=MESH,
        ).start()
        return 0

    lax.fori_loop(1, 32, send_potential, 0)
    keep = pltpu.make_async_copy(
        pbuf.at[pl.ds(pl.multiple_of(16 * r + 8 * half, 8), 8)], pl_in.at[slot], a2_loc
    )
    keep.start()

    def prepare(d):
        for rho in range(8):
            hi, lo = split(vl[32 * d:32 * d + 32, rho, :])
            vh[32 * d:32 * d + 32, 128 * rho:128 * rho + 128] = hi
            vlo[32 * d:32 * d + 32, 128 * rho:128 * rho + 128] = lo

    own.wait()
    wait_part(0, 1 - half, 0)
    prepare(0)
    prepare(1)
    relay(3)
    prepare(2)
    prepare(3)
    relay(4)
    prepare(4)

    keep.wait()
    rest = pl_in.at[pl.ds(0, 31)]
    pltpu.make_async_copy(rest, rest, a2_recv).wait()
    parts = [split(pl_in[:, rho, :]) for rho in range(8)]
    ph = jnp.concatenate([p[0] for p in parts], axis=1)
    plo = jnp.concatenate([p[1] for p in parts], axis=1)
    gram = dot_nt(ph, vh[...]) + dot_nt(plo, vh[...]) + dot_nt(ph, vlo[...])
    pad = jnp.zeros((16, 112), F32)
    sb[0:16, 0, :] = gram[0:16, 0:128]
    sb[0:16, 1, :] = jnp.concatenate([gram[0:16, 128:144], pad], axis=1)
    sb[16:32, 0, :] = gram[16:32, 16:144]
    sb[16:32, 1, :] = jnp.concatenate([gram[16:32, 144:160], pad], axis=1)

    def send_sum(i, _):
        p = lax.rem(me + i, 32)
        pltpu.make_async_remote_copy(
            sb.at[p], rl.at[me], r_send, r_recv,
            device_id=(base + p // 16, lax.rem(p, 16)), device_id_type=MESH,
        ).start()
        return 0

    lax.fori_loop(1, 32, send_sum, 0)
    keep = pltpu.make_async_copy(sb.at[me], rl.at[me], r_loc)
    keep.start()
    keep.wait()
    rest = rl.at[pl.ds(0, 31)]
    pltpu.make_async_copy(rest, rest, r_recv).wait()
    total = rl[0]
    for i in range(1, 32):
        total = total + rl[i]
    for s in range(9):
        out_ref[0, s:s + 1, :] = total[s // 8:s // 8 + 1, 16 * (s % 8):16 * (s % 8) + 16]

    for c in first:
        c.wait_send()
    for d in range(1, REACH):
        for k in range(2):
            part = half if k == 0 else 1 - half
            move(vl.at[pl.ds(32 * d + 16 * part, 16)], d + 1, part, 2 * d + 1 + k, down).wait_send()
    pltpu.make_async_copy(u, u, a1_send).wait()
    rest = pl_in.at[pl.ds(0, 31)]
    pltpu.make_async_copy(rest, rest, a2_send).wait()
    rest = rl.at[pl.ds(0, 31)]
    pltpu.make_async_copy(rest, rest, r_send).wait()


def body(fitting_vectors):
    ly, lyi, bz, bzi, kt, trig = constants()
    rows = fitting_vectors.reshape(16, 2, 8, 128).transpose(0, 2, 1, 3).reshape(16, 16, 128)
    any_spec = pl.BlockSpec(memory_space=pl.ANY)
    dma = pltpu.SemaphoreType.DMA
    return pl.pallas_call(
        functools.partial(body_kernel, trig),
        name="coulomb",
        out_shape=jax.ShapeDtypeStruct((1, 9, 16), F32),
        in_specs=[any_spec] * 6,
        out_specs=pl.BlockSpec(memory_space=pltpu.VMEM),
        scratch_shapes=[
            pltpu.VMEM((256, 128), F32),
            pltpu.VMEM((256, 128), F32),
            pltpu.VMEM((32, 8, 128), F32),
            pltpu.VMEM((160, 8, 128), F32),
            pltpu.VMEM(ly.shape, BF16),
            pltpu.VMEM(lyi.shape, BF16),
            pltpu.VMEM(bz.shape, BF16),
            pltpu.VMEM(bzi.shape, BF16),
            pltpu.VMEM(kt.shape, F32),
            pltpu.VMEM((96, 2048), BF16),
            pltpu.VMEM((512, 256), BF16),
            pltpu.VMEM((512, 256), BF16),
            pltpu.VMEM((512, 512), BF16),
            pltpu.VMEM((512, 512), BF16),
            pltpu.VMEM((192, 2048), BF16),
            pltpu.VMEM((32, 2048), F32),
            pltpu.VMEM((160, 1024), BF16),
            pltpu.VMEM((160, 1024), BF16),
            pltpu.VMEM((32, 2, 128), F32),
            pltpu.VMEM((32, 2, 128), F32),
            dma((5,)),
            dma, dma,
            dma((9,)), dma((9,)), dma,
            dma, dma, dma,
            dma, dma, dma,
        ],
        compiler_params=pltpu.CompilerParams(collective_id=0, has_side_effects=True),
    )(rows, ly, lyi, bz, bzi, kt)


def solution(mesh):
    return jax.shard_map(
        body,
        mesh=mesh,
        in_specs=(P("vec", "grid", None),),
        out_specs=P(("vec", "grid"), None, None),
        check_vma=False,
    )
```

```python
import functools
import math

import jax
import jax.numpy as jnp
import numpy as np
from jax import lax
from jax.experimental import pallas as pl
from jax.experimental.pallas import tpu as pltpu
from jax.sharding import PartitionSpec as P

N = 32
PAD = 2 * N
F32 = jnp.float32
BF16 = jnp.bfloat16
MESH = pl.DeviceIdType.MESH
REACH = 4
PIECES = 2
STEP = 16 // PIECES


def tables():
    pos = np.arange(N) - (N - 1) / 2.0
    freqs = np.concatenate([np.arange(N), np.arange(1, N + 1)])
    phase = 2.0 * np.pi * freqs[:, None] * pos[None, :] / PAD
    trig = np.where(np.arange(PAD)[:, None] < N, np.cos(phase), np.sin(phase))
    weight = np.where((freqs == 0) | (freqs == N), 1.0, 2.0)
    f = freqs.astype(np.float64)
    total = f[:, None, None] ** 2 + f[None, :, None] ** 2 + f[None, None, :] ** 2
    g2 = total * (2.0 * np.pi / PAD) ** 2
    safe = np.where(total > 0, g2, 1.0)
    kernel = 8.0 * np.pi * np.sin(np.sqrt(safe) * (N / 2)) ** 2 / safe
    kernel = np.where(total > 0, kernel, 2.0 * np.pi * N * N)
    kernel = kernel * weight[:, None, None] * weight[None, :, None] * weight[None, None, :]
    kernel = kernel / float(PAD) ** 3 / float(N) ** 3
    return trig, kernel


def split_np(a):
    hi = a.astype(np.float32).astype(BF16)
    lo = (a - hi.astype(np.float64)).astype(np.float32).astype(BF16)
    return hi, lo


def constants():
    trig, kernel = tables()
    row = np.arange(N)
    y_of_row = 4 * (row % 8) + row // 8
    ty = trig[:, y_of_row]
    hi, lo = split_np(ty)
    ly = np.concatenate([hi, hi, lo], axis=1)
    hi, lo = split_np(ty.T)
    lyi = np.concatenate([hi, hi, lo], axis=1)
    hi, lo = split_np(np.kron(np.eye(8), trig.T))
    bz = np.stack([hi, lo])
    hi, lo = split_np(np.kron(np.eye(4), trig))
    bzi = np.concatenate([hi, lo], axis=1)
    kt = kernel.reshape(8, 8, PAD, PAD).transpose(0, 2, 1, 3).reshape(8 * PAD, 8 * PAD)
    return ly, lyi, bz, bzi, kt.astype(np.float32), trig


def split(x):
    hi = x.astype(BF16)
    lo = (x - hi.astype(F32)).astype(BF16)
    return hi, lo


def dot(a, b):
    return jnp.dot(a, b, preferred_element_type=F32)


def dot_nt(a, b):
    return lax.dot_general(a, b, (((1,), (1,)), ((), ())), preferred_element_type=F32)


def combine(matrix, values):
    out = []
    for weights in matrix:
        acc = None
        for w, v in zip(weights, values):
            term = v * np.float32(w)
            acc = term if acc is None else acc + term
        out.append(acc)
    return out


def swap_chunks(tiles, odd1, odd2):
    t0, t1, t2, t3 = tiles

    def pair(a, b, mask, up, down):
        return (
            jnp.where(mask, pltpu.roll(b, up, 1), a),
            jnp.where(mask, b, pltpu.roll(a, down, 1)),
        )

    a0, a1 = pair(t0, t1, odd1, 32, 96)
    a2, a3 = pair(t2, t3, odd1, 32, 96)
    b0, b2 = pair(a0, a2, odd2, 64, 64)
    b1, b3 = pair(a1, a3, odd2, 64, 64)
    return b0, b1, b2, b3


def body_kernel(
    trig,
    v_in, ly_in, lyi_in, bz_in, bzi_in, kt_in,
    out_ref,
    u, pbuf, pl_in, vl, ly, lyi, bz, bzi, kt,
    m1, m2h, m2l, m3h, m3l, m4, m5, vh, vlo, sb, rl,
    c_sem, a1_send, a1_recv, v_send, v_recv, v_loc, a2_send, a2_recv, a2_loc, r_send, r_recv, r_loc,
):
    g = lax.axis_index("vec")
    r = lax.axis_index("grid")
    half = lax.rem(g, 2)
    sib = g + 1 - 2 * half
    down = lax.rem(g + 14, 16)
    down_sib = lax.rem(sib + 14, 16)
    up = lax.rem(g + 2, 16)
    up_sib = lax.rem(sib + 2, 16)

    me = 16 * half + r

    def turn(i):
        return lax.rem(r + i, 16)

    def others():
        for i in range(16):
            yield sib, 1 - half, turn(i)
            if i:
                yield g, half, turn(i)

    consts = [
        pltpu.make_async_copy(a, b, c_sem.at[i])
        for i, (a, b) in enumerate([(ly_in, ly), (lyi_in, lyi), (bz_in, bz), (bzi_in, bzi), (kt_in, kt)])
    ]
    for c in consts:
        c.start()
    own = pltpu.make_async_copy(
        v_in.at[:, pl.ds(pl.multiple_of(8 * half, 8), 8), :], vl.at[pl.ds(16 * half, 16)], v_loc
    )
    own.start()

    barrier = pltpu.get_barrier_semaphore()

    for i in range(16):
        pl.semaphore_signal(barrier, inc=1, device_id=(sib, turn(i)), device_id_type=MESH)
    for peer in (down, down_sib, up, up_sib):
        pl.semaphore_signal(barrier, inc=1, device_id=(peer, r), device_id_type=MESH)
    pl.semaphore_wait(barrier, 20)

    for i in range(16):
        m = turn(i)
        pltpu.make_async_remote_copy(
            v_in.at[m], u.at[pl.ds(pl.multiple_of(16 * r, 16), 16)], a1_send, a1_recv,
            device_id=(sib, m), device_id_type=MESH,
        ).start()

    def block(d, part, k):
        return vl.at[pl.ds(pl.multiple_of(32 * d + 16 * part + STEP * k, STEP), STEP)]

    def sem_of(d, far, k):
        return (2 * d + far) * PIECES + k

    def move(src, d, far, part, k, target):
        return pltpu.make_async_remote_copy(
            src, block(d, part, k), v_send.at[sem_of(d, far, k)], v_recv.at[sem_of(d, far, k)],
            device_id=(target, r), device_id_type=MESH,
        )

    def source(h, k):
        return v_in.at[pl.ds(STEP * k, STEP), pl.ds(pl.multiple_of(8 * h, 8), 8), :]

    first = [move(source(half, k), 1, 0, half, k, down) for k in range(PIECES)]
    first += [move(source(1 - half, k), 1, 1, half, k, down_sib) for k in range(PIECES)]
    first += [move(source(1 - half, k), 0, 1, half, k, sib) for k in range(PIECES)]
    for c in first:
        c.start()

    def part_of(far):
        return 1 - half if far else half

    def wait_block(d, far, k):
        ref = block(d, part_of(far), k)
        pltpu.make_async_copy(ref, ref, v_recv.at[sem_of(d, far, k)]).wait()

    def onward(d, far, k):
        return move(block(d, part_of(far), k), d + 1, far, part_of(far), k, down)

    def relay(d, far):
        for k in range(PIECES):
            wait_block(d, far, k)
            if d < REACH:
                onward(d, far, k).start()

    relay(1, 0)
    relay(1, 1)
    relay(2, 0)
    for c in consts:
        c.wait()
    pltpu.make_async_copy(u, u, a1_recv).wait()

    lane = lax.broadcasted_iota(jnp.int32, (8, 128), 1) // 32
    odd1 = lane % 2 == 1
    odd2 = lane >= 2

    def plane(x):
        return u[pl.ds(16 * (x // 2) + x % 2, 8, stride=2), :]

    low = [plane(15 - n) for n in range(16)]
    high = [plane(16 + n) for n in range(16)]
    for part in range(2):
        if part == 0:
            vals = [a + b for a, b in zip(high, low)]
        else:
            vals = [a - b for a, b in zip(high, low)]
        for a in range(8):
            q = 32 * part + 4 * a
            tiles = combine(trig[q:q + 4, 16:32], vals)
            tile = jnp.concatenate(swap_chunks(tiles, odd1, odd2), axis=0)
            hi, lo = split(tile)
            cols = pl.ds((8 * part + a) * 128, 128)
            m1[0:32, cols] = hi
            m1[32:64, cols] = lo
            m1[64:96, cols] = hi

    for n in range(8):
        hi, lo = split(dot(ly[...], m1[:, 256 * n:256 * n + 256]))
        m2h[64 * n:64 * n + 64, :] = hi
        m2l[64 * n:64 * n + 64, :] = lo

    for n in range(4):
        rows = slice(128 * n, 128 * n + 128)
        t = dot(m2h[rows, :], bz[0]) + dot(m2l[rows, :], bz[0]) + dot(m2h[rows, :], bz[1])
        hi, lo = split(t * kt[rows, :])
        m3h[rows, :] = hi
        m3l[rows, :] = lo

    relay(2, 1)
    relay(3, 0)

    for n in range(8):
        rows = slice(64 * n, 64 * n + 64)
        for h in range(2):
            cols = slice(256 * h, 256 * h + 256)
            w = dot(m3h[rows, cols], bzi[...])
            t = w[:, 0:128] + w[:, 128:256] + dot(m3l[rows, cols], bzi[:, 0:128])
            hi, lo = split(t)
            out = pl.ds((2 * n + h) * 128, 128)
            m4[0:64, out] = hi
            m4[64:128, out] = lo
            m4[128:192, out] = hi

    for n in range(8):
        cols = slice(256 * n, 256 * n + 256)
        m5[:, cols] = dot(lyi[...], m4[:, cols])

    sums = []
    for part in range(2):
        vals = []
        for a in range(8):
            cols = slice((8 * part + a) * 128, (8 * part + a) * 128 + 128)
            vals += swap_chunks([m5[8 * j:8 * j + 8, cols] for j in range(4)], odd1, odd2)
        sums.append(combine(trig[32 * part:32 * part + 32, 16:32].T, vals))
    for n in range(16):
        for x, val in ((16 + n, sums[0][n] + sums[1][n]), (15 - n, sums[0][n] - sums[1][n])):
            pbuf[pl.ds(16 * (x // 2) + x % 2, 8, stride=2), :] = val

    slot = (1 - half) * 16 + r

    for vec, h, m in others():
        rows = pl.multiple_of(16 * m + 8 * h, 8)
        pltpu.make_async_remote_copy(
            pbuf.at[pl.ds(rows, 8)], pl_in.at[slot], a2_send, a2_recv,
            device_id=(vec, m), device_id_type=MESH,
        ).start()
    keep = pltpu.make_async_copy(
        pbuf.at[pl.ds(pl.multiple_of(16 * r + 8 * half, 8), 8)], pl_in.at[slot], a2_loc
    )
    keep.start()

    def prepare(d):
        for rho in range(8):
            hi, lo = split(vl[32 * d:32 * d + 32, rho, :])
            vh[32 * d:32 * d + 32, 128 * rho:128 * rho + 128] = hi
            vlo[32 * d:32 * d + 32, 128 * rho:128 * rho + 128] = lo

    relay(3, 1)
    own.wait()
    for k in range(PIECES):
        wait_block(0, 1, k)
    for d in range(REACH):
        prepare(d)
    relay(REACH, 0)
    relay(REACH, 1)
    prepare(REACH)

    keep.wait()
    rest = pl_in.at[pl.ds(0, 31)]
    pltpu.make_async_copy(rest, rest, a2_recv).wait()
    parts = [split(pl_in[:, rho, :]) for rho in range(8)]
    ph = jnp.concatenate([p[0] for p in parts], axis=1)
    plo = jnp.concatenate([p[1] for p in parts], axis=1)
    gram = dot_nt(ph, vh[...]) + dot_nt(plo, vh[...]) + dot_nt(ph, vlo[...])
    pad = jnp.zeros((16, 112), F32)
    sb[0:16, 0, :] = gram[0:16, 0:128]
    sb[0:16, 1, :] = jnp.concatenate([gram[0:16, 128:144], pad], axis=1)
    sb[16:32, 0, :] = gram[16:32, 16:144]
    sb[16:32, 1, :] = jnp.concatenate([gram[16:32, 144:160], pad], axis=1)

    for vec, h, m in others():
        pltpu.make_async_remote_copy(
            sb.at[16 * h + m], rl.at[me], r_send, r_recv, device_id=(vec, m), device_id_type=MESH
        ).start()
    keep = pltpu.make_async_copy(sb.at[me], rl.at[me], r_loc)
    keep.start()
    keep.wait()
    rest = rl.at[pl.ds(0, 31)]
    pltpu.make_async_copy(rest, rest, r_recv).wait()
    total = rl[0]
    for i in range(1, 32):
        total = total + rl[i]
    for s in range(9):
        out_ref[s] = total[s // 8:s // 8 + 1, 16 * (s % 8):16 * (s % 8) + 16]

    for c in first:
        c.wait_send()
    for d in range(1, REACH):
        for far in range(2):
            for k in range(PIECES):
                onward(d, far, k).wait_send()
    pltpu.make_async_copy(u, u, a1_send).wait()
    rest = pl_in.at[pl.ds(0, 31)]
    pltpu.make_async_copy(rest, rest, a2_send).wait()
    rest = rl.at[pl.ds(0, 31)]
    pltpu.make_async_copy(rest, rest, r_send).wait()


def body(fitting_vectors):
    ly, lyi, bz, bzi, kt, trig = constants()
    rows = fitting_vectors.reshape(16, 2, 8, 128).transpose(0, 2, 1, 3).reshape(16, 16, 128)
    any_spec = pl.BlockSpec(memory_space=pl.ANY)
    dma = pltpu.SemaphoreType.DMA
    out = pl.pallas_call(
        functools.partial(body_kernel, trig),
        name="coulomb",
        out_shape=jax.ShapeDtypeStruct((9, 1, 16), F32),
        in_specs=[any_spec] * 6,
        out_specs=pl.BlockSpec(memory_space=pltpu.VMEM),
        scratch_shapes=[
            pltpu.VMEM((256, 128), F32),
            pltpu.VMEM((256, 128), F32),
            pltpu.VMEM((32, 8, 128), F32),
            pltpu.VMEM((160, 8, 128), F32),
            pltpu.VMEM(ly.shape, BF16),
            pltpu.VMEM(lyi.shape, BF16),
            pltpu.VMEM(bz.shape, BF16),
            pltpu.VMEM(bzi.shape, BF16),
            pltpu.VMEM(kt.shape, F32),
            pltpu.VMEM((96, 2048), BF16),
            pltpu.VMEM((512, 256), BF16),
            pltpu.VMEM((512, 256), BF16),
            pltpu.VMEM((512, 512), BF16),
            pltpu.VMEM((512, 512), BF16),
            pltpu.VMEM((192, 2048), BF16),
            pltpu.VMEM((32, 2048), F32),
            pltpu.VMEM((160, 1024), BF16),
            pltpu.VMEM((160, 1024), BF16),
            pltpu.VMEM((32, 2, 128), F32),
            pltpu.VMEM((32, 2, 128), F32),
            dma((5,)),
            dma, dma,
            dma((10 * PIECES,)), dma((10 * PIECES,)), dma,
            dma, dma, dma,
            dma, dma, dma,
        ],
        compiler_params=pltpu.CompilerParams(collective_id=0, has_side_effects=True),
    )(rows, ly, lyi, bz, bzi, kt)
    return out.transpose(1, 0, 2)


def solution(mesh):
    return jax.shard_map(
        body,
        mesh=mesh,
        in_specs=(P("vec", "grid", None),),
        out_specs=P(("vec", "grid"), None, None),
        check_vma=False,
    )
```

```python
import functools
import math

import jax
import jax.numpy as jnp
import numpy as np
from jax import lax
from jax.experimental import pallas as pl
from jax.experimental.pallas import tpu as pltpu
from jax.sharding import PartitionSpec as P

N = 32
PAD = 2 * N
F32 = jnp.float32
BF16 = jnp.bfloat16
MESH = pl.DeviceIdType.MESH
REACH = 4
PIECES = 2
STEP = 16 // PIECES
BEFORE = 8
MIDDLE = 8


def tables():
    pos = np.arange(N) - (N - 1) / 2.0
    freqs = np.concatenate([np.arange(N), np.arange(1, N + 1)])
    phase = 2.0 * np.pi * freqs[:, None] * pos[None, :] / PAD
    trig = np.where(np.arange(PAD)[:, None] < N, np.cos(phase), np.sin(phase))
    weight = np.where((freqs == 0) | (freqs == N), 1.0, 2.0)
    f = freqs.astype(np.float64)
    total = f[:, None, None] ** 2 + f[None, :, None] ** 2 + f[None, None, :] ** 2
    g2 = total * (2.0 * np.pi / PAD) ** 2
    safe = np.where(total > 0, g2, 1.0)
    kernel = 8.0 * np.pi * np.sin(np.sqrt(safe) * (N / 2)) ** 2 / safe
    kernel = np.where(total > 0, kernel, 2.0 * np.pi * N * N)
    kernel = kernel * weight[:, None, None] * weight[None, :, None] * weight[None, None, :]
    kernel = kernel / float(PAD) ** 3 / float(N) ** 3
    return trig, kernel


def split_np(a):
    hi = a.astype(np.float32).astype(BF16)
    lo = (a - hi.astype(np.float64)).astype(np.float32).astype(BF16)
    return hi, lo


def constants():
    trig, kernel = tables()
    row = np.arange(N)
    y_of_row = 4 * (row % 8) + row // 8
    ty = trig[:, y_of_row]
    hi, lo = split_np(ty)
    ly = np.concatenate([hi, hi, lo], axis=1)
    hi, lo = split_np(ty.T)
    lyi = np.concatenate([hi, hi, lo], axis=1)
    hi, lo = split_np(np.kron(np.eye(8), trig.T))
    bz = np.stack([hi, lo])
    hi, lo = split_np(np.kron(np.eye(4), trig))
    bzi = np.concatenate([hi, lo], axis=1)
    kt = kernel.reshape(8, 8, PAD, PAD).transpose(0, 2, 1, 3).reshape(8 * PAD, 8 * PAD)
    return ly, lyi, bz, bzi, kt.astype(np.float32), trig


def split(x):
    hi = x.astype(BF16)
    lo = (x - hi.astype(F32)).astype(BF16)
    return hi, lo


def dot(a, b):
    return jnp.dot(a, b, preferred_element_type=F32)


def dot_nt(a, b):
    return lax.dot_general(a, b, (((1,), (1,)), ((), ())), preferred_element_type=F32)


def combine(matrix, values):
    out = []
    for weights in matrix:
        acc = None
        for w, v in zip(weights, values):
            term = v * np.float32(w)
            acc = term if acc is None else acc + term
        out.append(acc)
    return out


def swap_chunks(tiles, odd1, odd2):
    t0, t1, t2, t3 = tiles

    def pair(a, b, mask, up, down):
        return (
            jnp.where(mask, pltpu.roll(b, up, 1), a),
            jnp.where(mask, b, pltpu.roll(a, down, 1)),
        )

    a0, a1 = pair(t0, t1, odd1, 32, 96)
    a2, a3 = pair(t2, t3, odd1, 32, 96)
    b0, b2 = pair(a0, a2, odd2, 64, 64)
    b1, b3 = pair(a1, a3, odd2, 64, 64)
    return b0, b1, b2, b3


def body_kernel(
    trig,
    v_in, ly_in, lyi_in, bz_in, bzi_in, kt_in,
    out_ref,
    u, pbuf, pl_in, vl, ly, lyi, bz, bzi, kt,
    m1, m2h, m2l, m3h, m3l, m4, m5, vh, vlo, sb, rl,
    c_sem, a1_send, a1_recv, v_send, v_recv, v_loc, a2_send, a2_recv, a2_loc, r_send, r_recv, r_loc,
):
    g = lax.axis_index("vec")
    r = lax.axis_index("grid")
    half = lax.rem(g, 2)
    sib = g + 1 - 2 * half
    down = lax.rem(g + 14, 16)
    down_sib = lax.rem(sib + 14, 16)
    up = lax.rem(g + 2, 16)
    up_sib = lax.rem(sib + 2, 16)

    me = 16 * half + r

    def turn(i):
        return lax.rem(r + i, 16)

    def others():
        for i in range(16):
            yield sib, 1 - half, turn(i)
            if i:
                yield g, half, turn(i)

    consts = [
        pltpu.make_async_copy(a, b, c_sem.at[i])
        for i, (a, b) in enumerate([(ly_in, ly), (lyi_in, lyi), (bz_in, bz), (bzi_in, bzi), (kt_in, kt)])
    ]
    for c in consts:
        c.start()
    own = pltpu.make_async_copy(
        v_in.at[:, pl.ds(pl.multiple_of(8 * half, 8), 8), :], vl.at[pl.ds(16 * half, 16)], v_loc
    )
    own.start()

    barrier = pltpu.get_barrier_semaphore()

    for i in range(16):
        pl.semaphore_signal(barrier, inc=1, device_id=(sib, turn(i)), device_id_type=MESH)
    for peer in (down, down_sib, up, up_sib):
        pl.semaphore_signal(barrier, inc=1, device_id=(peer, r), device_id_type=MESH)
    @pl.when(g < 2)
    def _():
        for peer in (g, sib):
            pl.semaphore_signal(barrier, inc=1, device_id=(peer + 8, r), device_id_type=MESH)

    early = jnp.where(jnp.logical_and(g >= 8, g < 10), 2, 0)
    pl.semaphore_wait(barrier, 20 + early)

    for i in range(16):
        m = turn(i)
        pltpu.make_async_remote_copy(
            v_in.at[m], u.at[pl.ds(pl.multiple_of(16 * r, 16), 16)], a1_send, a1_recv,
            device_id=(sib, m), device_id_type=MESH,
        ).start()

    def block(d, part, k):
        return vl.at[pl.ds(pl.multiple_of(32 * d + 16 * part + STEP * k, STEP), STEP)]

    def sem_of(d, far, k):
        return (2 * d + far) * PIECES + k

    def move(src, d, far, part, k, target, leave=0):
        return pltpu.make_async_remote_copy(
            src, block(d, part, k), v_send.at[sem_of(d + leave, far, k)], v_recv.at[sem_of(d, far, k)],
            device_id=(target, r), device_id_type=MESH,
        )

    def source(h, k):
        return v_in.at[pl.ds(STEP * k, STEP), pl.ds(pl.multiple_of(8 * h, 8), 8), :]

    first = []
    for k in range(PIECES):
        first.append(move(source(half, k), 1, 0, half, k, down))
        first.append(move(source(1 - half, k), 1, 1, half, k, down_sib))
    first += [move(source(1 - half, k), 0, 1, half, k, sib) for k in range(PIECES)]
    plane = g // 2
    late = jnp.logical_and(plane >= 4, plane <= 4)
    passes = jnp.logical_or(plane < 1, plane > 1)
    direct = []
    for k in range(PIECES):
        direct.append(move(source(half, k), REACH, 0, half, k, lax.rem(g + 8, 16), 1))
        direct.append(move(source(1 - half, k), REACH, 1, half, k, lax.rem(sib + 8, 16), 1))

    for c in first[:2 * PIECES]:
        c.start()

    @pl.when(late)
    def _():
        for c in direct:
            c.start()

    for c in first[2 * PIECES:]:
        c.start()

    def part_of(far):
        return 1 - half if far else half

    def wait_block(d, far, k):
        ref = block(d, part_of(far), k)
        pltpu.make_async_copy(ref, ref, v_recv.at[sem_of(d, far, k)]).wait()

    def onward(d, far, k):
        return move(block(d, part_of(far), k), d + 1, far, part_of(far), k, down)

    hops = iter([(d, far, k) for d in range(1, REACH) for k in range(PIECES) for far in range(2)])

    def relay(count):
        for _ in range(count * 2 * PIECES // 8):
            hop = next(hops)
            wait_block(*hop)
            if hop[0] < REACH - 1:
                onward(*hop).start()
            else:
                pl.when(passes)(onward(*hop).start)

    relay(BEFORE)
    for c in consts:
        c.wait()
    pltpu.make_async_copy(u, u, a1_recv).wait()

    lane = lax.broadcasted_iota(jnp.int32, (8, 128), 1) // 32
    odd1 = lane % 2 == 1
    odd2 = lane >= 2

    def slice_at(x):
        return u[pl.ds(16 * (x // 2) + x % 2, 8, stride=2), :]

    low = [slice_at(15 - n) for n in range(16)]
    high = [slice_at(16 + n) for n in range(16)]
    for part in range(2):
        if part == 0:
            vals = [a + b for a, b in zip(high, low)]
        else:
            vals = [a - b for a, b in zip(high, low)]
        for a in range(8):
            q = 32 * part + 4 * a
            tiles = combine(trig[q:q + 4, 16:32], vals)
            tile = jnp.concatenate(swap_chunks(tiles, odd1, odd2), axis=0)
            hi, lo = split(tile)
            cols = pl.ds((8 * part + a) * 128, 128)
            m1[0:32, cols] = hi
            m1[32:64, cols] = lo
            m1[64:96, cols] = hi

    for n in range(8):
        hi, lo = split(dot(ly[...], m1[:, 256 * n:256 * n + 256]))
        m2h[64 * n:64 * n + 64, :] = hi
        m2l[64 * n:64 * n + 64, :] = lo

    for n in range(4):
        rows = slice(128 * n, 128 * n + 128)
        t = dot(m2h[rows, :], bz[0]) + dot(m2l[rows, :], bz[0]) + dot(m2h[rows, :], bz[1])
        hi, lo = split(t * kt[rows, :])
        m3h[rows, :] = hi
        m3l[rows, :] = lo

    relay(MIDDLE)

    for n in range(8):
        rows = slice(64 * n, 64 * n + 64)
        for h in range(2):
            cols = slice(256 * h, 256 * h + 256)
            w = dot(m3h[rows, cols], bzi[...])
            t = w[:, 0:128] + w[:, 128:256] + dot(m3l[rows, cols], bzi[:, 0:128])
            hi, lo = split(t)
            out = pl.ds((2 * n + h) * 128, 128)
            m4[0:64, out] = hi
            m4[64:128, out] = lo
            m4[128:192, out] = hi

    for n in range(8):
        cols = slice(256 * n, 256 * n + 256)
        m5[:, cols] = dot(lyi[...], m4[:, cols])

    sums = []
    for part in range(2):
        vals = []
        for a in range(8):
            cols = slice((8 * part + a) * 128, (8 * part + a) * 128 + 128)
            vals += swap_chunks([m5[8 * j:8 * j + 8, cols] for j in range(4)], odd1, odd2)
        sums.append(combine(trig[32 * part:32 * part + 32, 16:32].T, vals))
    for n in range(16):
        for x, val in ((16 + n, sums[0][n] + sums[1][n]), (15 - n, sums[0][n] - sums[1][n])):
            pbuf[pl.ds(16 * (x // 2) + x % 2, 8, stride=2), :] = val

    slot = (1 - half) * 16 + r

    for vec, h, m in others():
        rows = pl.multiple_of(16 * m + 8 * h, 8)
        pltpu.make_async_remote_copy(
            pbuf.at[pl.ds(rows, 8)], pl_in.at[slot], a2_send, a2_recv,
            device_id=(vec, m), device_id_type=MESH,
        ).start()
    keep = pltpu.make_async_copy(
        pbuf.at[pl.ds(pl.multiple_of(16 * r + 8 * half, 8), 8)], pl_in.at[slot], a2_loc
    )
    keep.start()

    def prepare(d):
        for rho in range(8):
            hi, lo = split(vl[32 * d:32 * d + 32, rho, :])
            vh[32 * d:32 * d + 32, 128 * rho:128 * rho + 128] = hi
            vlo[32 * d:32 * d + 32, 128 * rho:128 * rho + 128] = lo

    relay(24 - BEFORE - MIDDLE)
    own.wait()
    for k in range(PIECES):
        wait_block(0, 1, k)
    for d in range(REACH):
        prepare(d)
    for k in range(PIECES):
        wait_block(REACH, 0, k)
        wait_block(REACH, 1, k)
    prepare(REACH)

    keep.wait()
    rest = pl_in.at[pl.ds(0, 31)]
    pltpu.make_async_copy(rest, rest, a2_recv).wait()
    parts = [split(pl_in[:, rho, :]) for rho in range(8)]
    ph = jnp.concatenate([p[0] for p in parts], axis=1)
    plo = jnp.concatenate([p[1] for p in parts], axis=1)
    gram = dot_nt(ph, vh[...]) + dot_nt(plo, vh[...]) + dot_nt(ph, vlo[...])
    pad = jnp.zeros((16, 112), F32)
    sb[0:16, 0, :] = gram[0:16, 0:128]
    sb[0:16, 1, :] = jnp.concatenate([gram[0:16, 128:144], pad], axis=1)
    sb[16:32, 0, :] = gram[16:32, 16:144]
    sb[16:32, 1, :] = jnp.concatenate([gram[16:32, 144:160], pad], axis=1)

    for vec, h, m in others():
        pltpu.make_async_remote_copy(
            sb.at[16 * h + m], rl.at[me], r_send, r_recv, device_id=(vec, m), device_id_type=MESH
        ).start()
    keep = pltpu.make_async_copy(sb.at[me], rl.at[me], r_loc)
    keep.start()
    keep.wait()
    rest = rl.at[pl.ds(0, 31)]
    pltpu.make_async_copy(rest, rest, r_recv).wait()
    total = rl[0]
    for i in range(1, 32):
        total = total + rl[i]
    for s in range(9):
        out_ref[s] = total[s // 8:s // 8 + 1, 16 * (s % 8):16 * (s % 8) + 16]

    for c in first:
        c.wait_send()

    @pl.when(late)
    def _():
        for c in direct:
            c.wait_send()

    for d in range(1, REACH):
        for far in range(2):
            for k in range(PIECES):
                if d < REACH - 1:
                    onward(d, far, k).wait_send()
                else:
                    pl.when(passes)(onward(d, far, k).wait_send)
    pltpu.make_async_copy(u, u, a1_send).wait()
    rest = pl_in.at[pl.ds(0, 31)]
    pltpu.make_async_copy(rest, rest, a2_send).wait()
    rest = rl.at[pl.ds(0, 31)]
    pltpu.make_async_copy(rest, rest, r_send).wait()


def body(fitting_vectors):
    ly, lyi, bz, bzi, kt, trig = constants()
    rows = fitting_vectors.reshape(16, 2, 8, 128).transpose(0, 2, 1, 3).reshape(16, 16, 128)
    any_spec = pl.BlockSpec(memory_space=pl.ANY)
    dma = pltpu.SemaphoreType.DMA
    out = pl.pallas_call(
        functools.partial(body_kernel, trig),
        name="coulomb",
        out_shape=jax.ShapeDtypeStruct((9, 1, 16), F32),
        in_specs=[any_spec] * 6,
        out_specs=pl.BlockSpec(memory_space=pltpu.VMEM),
        scratch_shapes=[
            pltpu.VMEM((256, 128), F32),
            pltpu.VMEM((256, 128), F32),
            pltpu.VMEM((32, 8, 128), F32),
            pltpu.VMEM((160, 8, 128), F32),
            pltpu.VMEM(ly.shape, BF16),
            pltpu.VMEM(lyi.shape, BF16),
            pltpu.VMEM(bz.shape, BF16),
            pltpu.VMEM(bzi.shape, BF16),
            pltpu.VMEM(kt.shape, F32),
            pltpu.VMEM((96, 2048), BF16),
            pltpu.VMEM((512, 256), BF16),
            pltpu.VMEM((512, 256), BF16),
            pltpu.VMEM((512, 512), BF16),
            pltpu.VMEM((512, 512), BF16),
            pltpu.VMEM((192, 2048), BF16),
            pltpu.VMEM((32, 2048), F32),
            pltpu.VMEM((160, 1024), BF16),
            pltpu.VMEM((160, 1024), BF16),
            pltpu.VMEM((32, 2, 128), F32),
            pltpu.VMEM((32, 2, 128), F32),
            dma((5,)),
            dma, dma,
            dma((12 * PIECES,)), dma((10 * PIECES,)), dma,
            dma, dma, dma,
            dma, dma, dma,
        ],
        compiler_params=pltpu.CompilerParams(collective_id=0, has_side_effects=True),
    )(rows, ly, lyi, bz, bzi, kt)
    return out.transpose(1, 0, 2)


def solution(mesh):
    return jax.shard_map(
        body,
        mesh=mesh,
        in_specs=(P("vec", "grid", None),),
        out_specs=P(("vec", "grid"), None, None),
        check_vma=False,
    )
```

```python
import functools
import math

import jax
import jax.numpy as jnp
import numpy as np
from jax import lax
from jax.experimental import pallas as pl
from jax.experimental.pallas import tpu as pltpu
from jax.sharding import PartitionSpec as P

N = 32
PAD = 2 * N
F32 = jnp.float32
BF16 = jnp.bfloat16
MESH = pl.DeviceIdType.MESH
REACH = 4
PIECES = 4
STEP = 16 // PIECES
BEFORE = 12
MIDDLE = 4


def tables():
    pos = np.arange(N) - (N - 1) / 2.0
    freqs = np.concatenate([np.arange(N), np.arange(1, N + 1)])
    phase = 2.0 * np.pi * freqs[:, None] * pos[None, :] / PAD
    trig = np.where(np.arange(PAD)[:, None] < N, np.cos(phase), np.sin(phase))
    weight = np.where((freqs == 0) | (freqs == N), 1.0, 2.0)
    f = freqs.astype(np.float64)
    total = f[:, None, None] ** 2 + f[None, :, None] ** 2 + f[None, None, :] ** 2
    g2 = total * (2.0 * np.pi / PAD) ** 2
    safe = np.where(total > 0, g2, 1.0)
    kernel = 8.0 * np.pi * np.sin(np.sqrt(safe) * (N / 2)) ** 2 / safe
    kernel = np.where(total > 0, kernel, 2.0 * np.pi * N * N)
    kernel = kernel * weight[:, None, None] * weight[None, :, None] * weight[None, None, :]
    kernel = kernel / float(PAD) ** 3 / float(N) ** 3
    return trig, kernel


def split_np(a):
    hi = a.astype(np.float32).astype(BF16)
    lo = (a - hi.astype(np.float64)).astype(np.float32).astype(BF16)
    return hi, lo


def constants():
    trig, kernel = tables()
    row = np.arange(N)
    y_of_row = 4 * (row % 8) + row // 8
    ty = trig[:, y_of_row]
    hi, lo = split_np(ty)
    ly = np.concatenate([hi, hi, lo], axis=1)
    hi, lo = split_np(ty.T)
    lyi = np.concatenate([hi, hi, lo], axis=1)
    hi, lo = split_np(np.kron(np.eye(8), trig.T))
    bz = np.stack([hi, lo])
    hi, lo = split_np(np.kron(np.eye(4), trig))
    bzi = np.concatenate([hi, lo], axis=1)
    kt = kernel.reshape(8, 8, PAD, PAD).transpose(0, 2, 1, 3).reshape(8 * PAD, 8 * PAD)
    return ly, lyi, bz, bzi, kt.astype(np.float32), trig


def split(x):
    hi = x.astype(BF16)
    lo = (x - hi.astype(F32)).astype(BF16)
    return hi, lo


def dot(a, b):
    return jnp.dot(a, b, preferred_element_type=F32)


def dot_nt(a, b):
    return lax.dot_general(a, b, (((1,), (1,)), ((), ())), preferred_element_type=F32)


def combine(matrix, values):
    out = []
    for weights in matrix:
        acc = None
        for w, v in zip(weights, values):
            term = v * np.float32(w)
            acc = term if acc is None else acc + term
        out.append(acc)
    return out


def swap_chunks(tiles, odd1, odd2):
    t0, t1, t2, t3 = tiles

    def pair(a, b, mask, up, down):
        return (
            jnp.where(mask, pltpu.roll(b, up, 1), a),
            jnp.where(mask, b, pltpu.roll(a, down, 1)),
        )

    a0, a1 = pair(t0, t1, odd1, 32, 96)
    a2, a3 = pair(t2, t3, odd1, 32, 96)
    b0, b2 = pair(a0, a2, odd2, 64, 64)
    b1, b3 = pair(a1, a3, odd2, 64, 64)
    return b0, b1, b2, b3


def body_kernel(
    trig,
    v_in, ly_in, lyi_in, bz_in, bzi_in, kt_in,
    rl,
    u, pbuf, pl_in, vl, ly, lyi, bz, bzi, kt,
    m1, m2h, m2l, m3h, m3l, m4, m5, vh, vlo, sb,
    ready, ready_up, c_sem, a1_send, a1_recv, v_send, v_recv, v_loc, a2_send, a2_recv, a2_loc, r_send, r_recv, r_loc,
):
    g = lax.axis_index("vec")
    r = lax.axis_index("grid")
    half = lax.rem(g, 2)
    sib = g + 1 - 2 * half
    down = lax.rem(g + 14, 16)
    down_sib = lax.rem(sib + 14, 16)
    up = lax.rem(g + 2, 16)
    up_sib = lax.rem(sib + 2, 16)

    me = 16 * half + r

    def turn(i):
        return lax.rem(r + i, 16)

    def others():
        for i in range(16):
            yield sib, 1 - half, turn(i)
            if i:
                yield g, half, turn(i)

    plane = g // 2
    barrier = pltpu.get_barrier_semaphore()

    def rank(x, y_hi, parity):
        return 2 * (jnp.minimum(x, 2) + jnp.minimum(2 * y_hi + parity, 2)) + parity

    my_rank = rank(r // 4, lax.rem(r, 4) // 2, half)
    later = [
        (m, (rank(m // 4, m % 4 // 2, 1 - half) > my_rank).astype(jnp.int32)) for m in range(16)
    ]
    n_later = functools.reduce(lambda a, b: a + b, [after for _, after in later])

    def greet(sem, vec, to):
        pl.semaphore_signal(sem, inc=1, device_id=(vec, to), device_id_type=MESH)

    greet(barrier, g, r + 1 - 2 * lax.rem(r, 2))

    @pl.when(plane < 7)
    def _():
        greet(barrier, up, r)
        greet(barrier, up_sib, r)

    for m, after in later:
        pl.when(after == 1)(functools.partial(greet, barrier, sib, m))

    @pl.when(plane == 0)
    def _():
        for away in (8, 14):
            greet(barrier, g + away, r)
            greet(barrier, sib + away, r)

    consts = [
        pltpu.make_async_copy(a, b, c_sem.at[i])
        for i, (a, b) in enumerate([(ly_in, ly), (lyi_in, lyi), (bz_in, bz), (bzi_in, bzi), (kt_in, kt)])
    ]
    for c in consts:
        c.start()
    own = pltpu.make_async_copy(
        v_in.at[:, pl.ds(pl.multiple_of(8 * half, 8), 8), :], vl.at[pl.ds(16 * half, 16)], v_loc
    )
    own.start()

    across = jnp.where(plane > 0, 2, 0) + jnp.where(jnp.logical_or(plane == 4, plane == 7), 2, 0)
    pl.semaphore_wait(barrier, 17 - n_later + across)

    for m, after in later:
        pl.when(after == 0)(functools.partial(greet, ready, sib, m))

    @pl.when(plane == 7)
    def _():
        greet(ready_up, up, r)
        greet(ready_up, up_sib, r)

    def block(d, part, k):
        return vl.at[pl.ds(pl.multiple_of(32 * d + 16 * part + STEP * k, STEP), STEP)]

    def sem_of(d, far, k):
        return (2 * d + far) * PIECES + k

    def move(src, d, far, part, k, target, leave=0):
        return pltpu.make_async_remote_copy(
            src, block(d, part, k), v_send.at[sem_of(d + leave, far, k)], v_recv.at[sem_of(d, far, k)],
            device_id=(target, r), device_id_type=MESH,
        )

    def source(h, k):
        return v_in.at[pl.ds(STEP * k, STEP), pl.ds(pl.multiple_of(8 * h, 8), 8), :]

    first = []
    for k in range(PIECES):
        first.append(move(source(half, k), 1, 0, half, k, down))
        first.append(move(source(1 - half, k), 1, 1, half, k, down_sib))
    first += [move(source(1 - half, k), 0, 1, half, k, sib) for k in range(PIECES)]
    passes = plane != 1
    direct = []
    for k in range(PIECES):
        direct.append(move(source(half, k), REACH, 0, half, k, lax.rem(g + 8, 16), 1))
        direct.append(move(source(1 - half, k), REACH, 1, half, k, lax.rem(sib + 8, 16), 1))

    def start_down():
        for c in first[:2 * PIECES]:
            c.start()

    pl.when(plane > 0)(start_down)

    @pl.when(plane == 4)
    def _():
        for c in direct:
            c.start()

    pl.when(n_later > 0)(lambda: pl.semaphore_wait(ready, n_later))

    for i in range(16):
        m = turn(i)
        pltpu.make_async_remote_copy(
            v_in.at[m], u.at[pl.ds(pl.multiple_of(16 * r, 16), 16)], a1_send, a1_recv,
            device_id=(sib, m), device_id_type=MESH,
        ).start()

    for c in first[2 * PIECES:]:
        c.start()

    @pl.when(plane == 0)
    def _():
        pl.semaphore_wait(ready_up, 2)
        start_down()

    def part_of(far):
        return 1 - half if far else half

    def wait_block(d, far, k):
        ref = block(d, part_of(far), k)
        pltpu.make_async_copy(ref, ref, v_recv.at[sem_of(d, far, k)]).wait()

    def onward(d, far, k):
        return move(block(d, part_of(far), k), d + 1, far, part_of(far), k, down)

    hops = iter([(d, far, k) for d in range(1, REACH) for k in range(PIECES) for far in range(2)])

    def relay(count):
        for _ in range(count * 2 * PIECES // 8):
            hop = next(hops)
            wait_block(*hop)
            if hop[0] < REACH - 1:
                onward(*hop).start()
            else:
                pl.when(passes)(onward(*hop).start)

    relay(BEFORE)
    for c in consts:
        c.wait()
    pltpu.make_async_copy(u, u, a1_recv).wait()

    lane = lax.broadcasted_iota(jnp.int32, (8, 128), 1) // 32
    odd1 = lane % 2 == 1
    odd2 = lane >= 2

    def slice_at(x):
        return u[pl.ds(16 * (x // 2) + x % 2, 8, stride=2), :]

    low = [slice_at(15 - n) for n in range(16)]
    high = [slice_at(16 + n) for n in range(16)]
    for part in range(2):
        if part == 0:
            vals = [a + b for a, b in zip(high, low)]
        else:
            vals = [a - b for a, b in zip(high, low)]
        for a in range(8):
            q = 32 * part + 4 * a
            tiles = combine(trig[q:q + 4, 16:32], vals)
            tile = jnp.concatenate(swap_chunks(tiles, odd1, odd2), axis=0)
            hi, lo = split(tile)
            cols = pl.ds((8 * part + a) * 128, 128)
            m1[0:32, cols] = hi
            m1[32:64, cols] = lo
            m1[64:96, cols] = hi

    for n in range(8):
        hi, lo = split(dot(ly[...], m1[:, 256 * n:256 * n + 256]))
        m2h[64 * n:64 * n + 64, :] = hi
        m2l[64 * n:64 * n + 64, :] = lo

    for n in range(4):
        rows = slice(128 * n, 128 * n + 128)
        t = dot(m2h[rows, :], bz[0]) + dot(m2l[rows, :], bz[0]) + dot(m2h[rows, :], bz[1])
        hi, lo = split(t * kt[rows, :])
        m3h[rows, :] = hi
        m3l[rows, :] = lo

    relay(MIDDLE)

    for n in range(8):
        rows = slice(64 * n, 64 * n + 64)
        for h in range(2):
            cols = slice(256 * h, 256 * h + 256)
            w = dot(m3h[rows, cols], bzi[...])
            t = w[:, 0:128] + w[:, 128:256] + dot(m3l[rows, cols], bzi[:, 0:128])
            hi, lo = split(t)
            out = pl.ds((2 * n + h) * 128, 128)
            m4[0:64, out] = hi
            m4[64:128, out] = lo
            m4[128:192, out] = hi

    for n in range(8):
        cols = slice(256 * n, 256 * n + 256)
        m5[:, cols] = dot(lyi[...], m4[:, cols])

    sums = []
    for part in range(2):
        vals = []
        for a in range(8):
            cols = slice((8 * part + a) * 128, (8 * part + a) * 128 + 128)
            vals += swap_chunks([m5[8 * j:8 * j + 8, cols] for j in range(4)], odd1, odd2)
        sums.append(combine(trig[32 * part:32 * part + 32, 16:32].T, vals))
    for n in range(16):
        for x, val in ((16 + n, sums[0][n] + sums[1][n]), (15 - n, sums[0][n] - sums[1][n])):
            pbuf[pl.ds(16 * (x // 2) + x % 2, 8, stride=2), :] = val

    slot = (1 - half) * 16 + r

    for vec, h, m in others():
        rows = pl.multiple_of(16 * m + 8 * h, 8)
        pltpu.make_async_remote_copy(
            pbuf.at[pl.ds(rows, 8)], pl_in.at[slot], a2_send, a2_recv,
            device_id=(vec, m), device_id_type=MESH,
        ).start()
    keep = pltpu.make_async_copy(
        pbuf.at[pl.ds(pl.multiple_of(16 * r + 8 * half, 8), 8)], pl_in.at[slot], a2_loc
    )
    keep.start()

    def prepare(d):
        for rho in range(8):
            hi, lo = split(vl[32 * d:32 * d + 32, rho, :])
            vh[32 * d:32 * d + 32, 128 * rho:128 * rho + 128] = hi
            vlo[32 * d:32 * d + 32, 128 * rho:128 * rho + 128] = lo

    relay(24 - BEFORE - MIDDLE)
    own.wait()
    for k in range(PIECES):
        wait_block(0, 1, k)
    for d in range(REACH):
        prepare(d)
    for k in range(PIECES):
        wait_block(REACH, 0, k)
        wait_block(REACH, 1, k)
    prepare(REACH)

    keep.wait()
    rest = pl_in.at[pl.ds(0, 31)]
    pltpu.make_async_copy(rest, rest, a2_recv).wait()
    parts = [split(pl_in[:, rho, :]) for rho in range(8)]
    ph = jnp.concatenate([p[0] for p in parts], axis=1)
    plo = jnp.concatenate([p[1] for p in parts], axis=1)
    gram = dot_nt(ph, vh[...]) + dot_nt(plo, vh[...]) + dot_nt(ph, vlo[...])
    pad = jnp.zeros((16, 112), F32)
    sb[0:16, 0, :] = gram[0:16, 0:128]
    sb[0:16, 1, :] = jnp.concatenate([gram[0:16, 128:144], pad], axis=1)
    sb[16:32, 0, :] = gram[16:32, 16:144]
    sb[16:32, 1, :] = jnp.concatenate([gram[16:32, 144:160], pad], axis=1)

    for vec, h, m in others():
        pltpu.make_async_remote_copy(
            sb.at[16 * h + m], rl.at[me], r_send, r_recv, device_id=(vec, m), device_id_type=MESH
        ).start()
    keep = pltpu.make_async_copy(sb.at[me], rl.at[me], r_loc)
    keep.start()
    keep.wait()
    rest = rl.at[pl.ds(0, 31)]
    pltpu.make_async_copy(rest, rest, r_recv).wait()
    for c in first:
        c.wait_send()

    @pl.when(plane == 4)
    def _():
        for c in direct:
            c.wait_send()

    for d in range(1, REACH):
        for far in range(2):
            for k in range(PIECES):
                if d < REACH - 1:
                    onward(d, far, k).wait_send()
                else:
                    pl.when(passes)(onward(d, far, k).wait_send)
    pltpu.make_async_copy(u, u, a1_send).wait()
    rest = pl_in.at[pl.ds(0, 31)]
    pltpu.make_async_copy(rest, rest, a2_send).wait()
    rest = rl.at[pl.ds(0, 31)]
    pltpu.make_async_copy(rest, rest, r_send).wait()


def finish(parts, out):
    total = jnp.sum(parts[...], axis=0)
    for s in range(9):
        out[s] = total[s // 8:s // 8 + 1, 16 * (s % 8):16 * (s % 8) + 16]


def body(fitting_vectors):
    ly, lyi, bz, bzi, kt, trig = constants()
    rows = fitting_vectors.reshape(16, 2, 8, 128).transpose(0, 2, 1, 3).reshape(16, 16, 128)
    any_spec = pl.BlockSpec(memory_space=pl.ANY)
    dma = pltpu.SemaphoreType.DMA
    partial = pl.pallas_call(
        functools.partial(body_kernel, trig),
        name="coulomb",
        out_shape=jax.ShapeDtypeStruct((32, 2, 128), F32),
        in_specs=[any_spec] * 6,
        out_specs=any_spec,
        scratch_shapes=[
            pltpu.VMEM((256, 128), F32),
            pltpu.VMEM((256, 128), F32),
            pltpu.VMEM((32, 8, 128), F32),
            pltpu.VMEM((160, 8, 128), F32),
            pltpu.VMEM(ly.shape, BF16),
            pltpu.VMEM(lyi.shape, BF16),
            pltpu.VMEM(bz.shape, BF16),
            pltpu.VMEM(bzi.shape, BF16),
            pltpu.VMEM(kt.shape, F32),
            pltpu.VMEM((96, 2048), BF16),
            pltpu.VMEM((512, 256), BF16),
            pltpu.VMEM((512, 256), BF16),
            pltpu.VMEM((512, 512), BF16),
            pltpu.VMEM((512, 512), BF16),
            pltpu.VMEM((192, 2048), BF16),
            pltpu.VMEM((32, 2048), F32),
            pltpu.VMEM((160, 1024), BF16),
            pltpu.VMEM((160, 1024), BF16),
            pltpu.VMEM((32, 2, 128), F32),
            pltpu.SemaphoreType.REGULAR,
            pltpu.SemaphoreType.REGULAR,
            dma((5,)),
            dma, dma,
            dma((12 * PIECES,)), dma((10 * PIECES,)), dma,
            dma, dma, dma,
            dma, dma, dma,
        ],
        compiler_params=pltpu.CompilerParams(collective_id=0, has_side_effects=True),
    )(rows, ly, lyi, bz, bzi, kt)
    out = pl.pallas_call(
        finish,
        name="finish",
        out_shape=jax.ShapeDtypeStruct((9, 1, 16), F32),
        in_specs=[pl.BlockSpec(memory_space=pltpu.VMEM)],
        out_specs=pl.BlockSpec(memory_space=pltpu.VMEM),
    )(partial)
    return out.transpose(1, 0, 2)


def solution(mesh):
    return jax.shard_map(
        body,
        mesh=mesh,
        in_specs=(P("vec", "grid", None),),
        out_specs=P(("vec", "grid"), None, None),
        check_vma=False,
    )
```

```python
import functools
import math

import jax
import jax.numpy as jnp
import numpy as np
from jax import lax
from jax.experimental import pallas as pl
from jax.experimental.pallas import tpu as pltpu
from jax.sharding import PartitionSpec as P

N = 32
PAD = 2 * N
F32 = jnp.float32
BF16 = jnp.bfloat16
MESH = pl.DeviceIdType.MESH
REACH = 4
PIECES = 2
STEP = 16 // PIECES
BEFORE = 12
MIDDLE = 4


def tables():
    pos = np.arange(N) - (N - 1) / 2.0
    freqs = np.concatenate([np.arange(N), np.arange(1, N + 1)])
    phase = 2.0 * np.pi * freqs[:, None] * pos[None, :] / PAD
    trig = np.where(np.arange(PAD)[:, None] < N, np.cos(phase), np.sin(phase))
    weight = np.where((freqs == 0) | (freqs == N), 1.0, 2.0)
    f = freqs.astype(np.float64)
    total = f[:, None, None] ** 2 + f[None, :, None] ** 2 + f[None, None, :] ** 2
    g2 = total * (2.0 * np.pi / PAD) ** 2
    safe = np.where(total > 0, g2, 1.0)
    kernel = 8.0 * np.pi * np.sin(np.sqrt(safe) * (N / 2)) ** 2 / safe
    kernel = np.where(total > 0, kernel, 2.0 * np.pi * N * N)
    kernel = kernel * weight[:, None, None] * weight[None, :, None] * weight[None, None, :]
    kernel = kernel / float(PAD) ** 3 / float(N) ** 3
    return trig, kernel


def split_np(a):
    hi = a.astype(np.float32).astype(BF16)
    lo = (a - hi.astype(np.float64)).astype(np.float32).astype(BF16)
    return hi, lo


def constants():
    trig, kernel = tables()
    row = np.arange(N)
    y_of_row = 4 * (row % 8) + row // 8
    ty = trig[:, y_of_row]
    hi, lo = split_np(ty)
    ly = np.concatenate([hi, hi, lo], axis=1)
    hi, lo = split_np(ty.T)
    lyi = np.concatenate([hi, hi, lo], axis=1)
    hi, lo = split_np(np.kron(np.eye(8), trig.T))
    bz = np.stack([hi, lo])
    hi, lo = split_np(np.kron(np.eye(4), trig))
    bzi = np.concatenate([hi, lo], axis=1)
    kt = kernel.reshape(8, 8, PAD, PAD).transpose(0, 2, 1, 3).reshape(8 * PAD, 8 * PAD)
    return ly, lyi, bz, bzi, kt.astype(np.float32), trig


def split(x):
    hi = x.astype(BF16)
    lo = (x - hi.astype(F32)).astype(BF16)
    return hi, lo


def dot(a, b):
    return jnp.dot(a, b, preferred_element_type=F32)


def dot_nt(a, b):
    return lax.dot_general(a, b, (((1,), (1,)), ((), ())), preferred_element_type=F32)


def combine(matrix, values):
    out = []
    for weights in matrix:
        acc = None
        for w, v in zip(weights, values):
            term = v * np.float32(w)
            acc = term if acc is None else acc + term
        out.append(acc)
    return out


def swap_chunks(tiles, odd1, odd2):
    t0, t1, t2, t3 = tiles

    def pair(a, b, mask, up, down):
        return (
            jnp.where(mask, pltpu.roll(b, up, 1), a),
            jnp.where(mask, b, pltpu.roll(a, down, 1)),
        )

    a0, a1 = pair(t0, t1, odd1, 32, 96)
    a2, a3 = pair(t2, t3, odd1, 32, 96)
    b0, b2 = pair(a0, a2, odd2, 64, 64)
    b1, b3 = pair(a1, a3, odd2, 64, 64)
    return b0, b1, b2, b3


def body_kernel(
    trig,
    v_in, ly_in, lyi_in, bz_in, bzi_in, kt_in,
    rl,
    u, pbuf, pl_in, vl, vp, ly, lyi, bz, bzi, kt,
    m1, m2h, m2l, m3h, m3l, m4, m5, vh, vlo, sb,
    ready, ready_up, c_sem, a1_send, a1_recv, v_send, v_recv, v_loc, a2_send, a2_recv, a2_loc, r_send, r_recv, r_loc,
):
    g = lax.axis_index("vec")
    r = lax.axis_index("grid")
    half = lax.rem(g, 2)
    sib = g + 1 - 2 * half
    down = lax.rem(g + 14, 16)
    down_sib = lax.rem(sib + 14, 16)
    up = lax.rem(g + 2, 16)
    up_sib = lax.rem(sib + 2, 16)

    me = 16 * half + r

    def turn(i):
        return lax.rem(r + i, 16)

    def others():
        for i in range(16):
            yield sib, 1 - half, turn(i)
            if i:
                yield g, half, turn(i)

    plane = g // 2
    barrier = pltpu.get_barrier_semaphore()

    def rank(x, y_hi, parity):
        return 2 * (jnp.minimum(x, 2) + jnp.minimum(2 * y_hi + parity, 2)) + parity

    my_rank = rank(r // 4, lax.rem(r, 4) // 2, half)
    later = [
        (m, (rank(m // 4, m % 4 // 2, 1 - half) > my_rank).astype(jnp.int32)) for m in range(16)
    ]
    n_later = functools.reduce(lambda a, b: a + b, [after for _, after in later])

    def greet(sem, vec, to):
        pl.semaphore_signal(sem, inc=1, device_id=(vec, to), device_id_type=MESH)

    greet(barrier, g, r + 1 - 2 * lax.rem(r, 2))

    @pl.when(plane < 7)
    def _():
        greet(barrier, up, r)
        greet(barrier, up_sib, r)

    for m, after in later:
        pl.when(after == 1)(functools.partial(greet, barrier, sib, m))

    @pl.when(plane == 0)
    def _():
        for away in (8, 14):
            greet(barrier, g + away, r)
            greet(barrier, sib + away, r)

    @pl.when(plane == 1)
    def _():
        for away in (4, 12):
            greet(barrier, g + away, r)
            greet(barrier, sib + away, r)

    @pl.when(plane == 2)
    def _():
        greet(barrier, g + 8, r)
        greet(barrier, sib + 8, r)

    @pl.when(plane == 7)
    def _():
        greet(barrier, g - 4, r)
        greet(barrier, sib - 4, r)

    consts = [
        pltpu.make_async_copy(a, b, c_sem.at[i])
        for i, (a, b) in enumerate([(ly_in, ly), (lyi_in, lyi), (bz_in, bz), (bzi_in, bzi), (kt_in, kt)])
    ]
    for c in consts:
        c.start()
    own = pltpu.make_async_copy(
        v_in.at[:, pl.ds(pl.multiple_of(8 * half, 8), 8), :], vl.at[pl.ds(16 * half, 16)], v_loc
    )
    own.start()

    across = jnp.where(plane > 0, 2, 0) + jnp.where(plane > 2, 2, 0) + jnp.where(plane == 7, 2, 0)
    pl.semaphore_wait(barrier, 17 - n_later + across)

    for m, after in later:
        pl.when(after == 0)(functools.partial(greet, ready, sib, m))

    @pl.when(plane == 7)
    def _():
        greet(ready_up, up, r)
        greet(ready_up, up_sib, r)

    @pl.when(plane == 3)
    def _():
        greet(ready_up, g - 4, r)
        greet(ready_up, sib - 4, r)

    def block(d, part, k):
        return vl.at[pl.ds(pl.multiple_of(32 * d + 16 * part + STEP * k, STEP), STEP)]

    def sem_of(d, far, k):
        return (2 * d + far) * PIECES + k

    def move(src, d, far, part, k, target, leave=0):
        return pltpu.make_async_remote_copy(
            src, block(d, part, k), v_send.at[sem_of(d + leave, far, k)], v_recv.at[sem_of(d, far, k)],
            device_id=(target, r), device_id_type=MESH,
        )

    def source(h, k):
        return v_in.at[pl.ds(STEP * k, STEP), pl.ds(pl.multiple_of(8 * h, 8), 8), :]

    first = []
    for k in range(PIECES):
        first.append(move(source(half, k), 1, 0, half, k, down))
        first.append(move(source(1 - half, k), 1, 1, half, k, down_sib))
    first += [move(source(1 - half, k), 0, 1, half, k, sib) for k in range(PIECES)]
    passes = jnp.logical_or(plane == 0, plane > 4)
    direct = []
    for k in range(PIECES):
        direct.append(move(source(half, k), REACH, 0, half, k, lax.rem(g + 8, 16), 1))
        direct.append(move(source(1 - half, k), REACH, 1, half, k, lax.rem(sib + 8, 16), 1))

    def pass_block(part, k):
        return vp.at[pl.ds(pl.multiple_of(16 * part + STEP * k, STEP), STEP)]

    def pass_up(far, k):
        vec = lax.rem((sib if far else g) + 4, 16)
        return pltpu.make_async_remote_copy(
            source(1 - half if far else half, k), pass_block(half, k),
            v_send.at[sem_of(REACH + 1, far, k)], v_recv.at[sem_of(REACH + 1, far, k)],
            device_id=(vec, r), device_id_type=MESH,
        )

    def pass_on(far, k):
        part = 1 - half if far else half
        return move(pass_block(part, k), REACH, far, part, k, lax.rem(g + 4, 16), 2)

    pieces = [(far, k) for k in range(PIECES) for far in range(2)]
    straight = jnp.logical_or(plane == 4, plane == 6)
    upward = jnp.logical_or(plane == 5, plane == 7)
    middle = jnp.logical_or(plane == 7, plane == 1)

    def relay_up():
        for far, k in pieces:
            ref = pass_block(1 - half if far else half, k)
            pltpu.make_async_copy(ref, ref, v_recv.at[sem_of(REACH + 1, far, k)]).wait()
            pass_on(far, k).start()

    def start_down():
        for c in first[:2 * PIECES]:
            c.start()

    pl.when(plane > 0)(start_down)

    @pl.when(straight)
    def _():
        for c in direct:
            c.start()

    @pl.when(upward)
    def _():
        for piece in pieces:
            pass_up(*piece).start()

    pl.when(n_later > 0)(lambda: pl.semaphore_wait(ready, n_later))

    for i in range(16):
        m = turn(i)
        pltpu.make_async_remote_copy(
            v_in.at[m], u.at[pl.ds(pl.multiple_of(16 * r, 16), 16)], a1_send, a1_recv,
            device_id=(sib, m), device_id_type=MESH,
        ).start()

    for c in first[2 * PIECES:]:
        c.start()

    @pl.when(plane == 0)
    def _():
        pl.semaphore_wait(ready_up, 2)
        start_down()

    @pl.when(plane == 1)
    def _():
        pl.semaphore_wait(ready_up, 2)

    def part_of(far):
        return 1 - half if far else half

    def wait_block(d, far, k):
        ref = block(d, part_of(far), k)
        pltpu.make_async_copy(ref, ref, v_recv.at[sem_of(d, far, k)]).wait()

    def onward(d, far, k):
        return move(block(d, part_of(far), k), d + 1, far, part_of(far), k, down)

    hops = iter([(d, far, k) for d in range(1, REACH) for k in range(PIECES) for far in range(2)])

    def relay(count):
        for _ in range(count * 2 * PIECES // 8):
            hop = next(hops)
            wait_block(*hop)
            if hop[0] < REACH - 1:
                onward(*hop).start()
            else:
                pl.when(passes)(onward(*hop).start)

    relay(BEFORE)
    pl.when(plane == 7)(relay_up)
    for c in consts:
        c.wait()
    pltpu.make_async_copy(u, u, a1_recv).wait()

    lane = lax.broadcasted_iota(jnp.int32, (8, 128), 1) // 32
    odd1 = lane % 2 == 1
    odd2 = lane >= 2

    def slice_at(x):
        return u[pl.ds(16 * (x // 2) + x % 2, 8, stride=2), :]

    low = [slice_at(15 - n) for n in range(16)]
    high = [slice_at(16 + n) for n in range(16)]
    for part in range(2):
        if part == 0:
            vals = [a + b for a, b in zip(high, low)]
        else:
            vals = [a - b for a, b in zip(high, low)]
        for a in range(8):
            q = 32 * part + 4 * a
            tiles = combine(trig[q:q + 4, 16:32], vals)
            tile = jnp.concatenate(swap_chunks(tiles, odd1, odd2), axis=0)
            hi, lo = split(tile)
            cols = pl.ds((8 * part + a) * 128, 128)
            m1[0:32, cols] = hi
            m1[32:64, cols] = lo
            m1[64:96, cols] = hi

    for n in range(8):
        hi, lo = split(dot(ly[...], m1[:, 256 * n:256 * n + 256]))
        m2h[64 * n:64 * n + 64, :] = hi
        m2l[64 * n:64 * n + 64, :] = lo

    for n in range(4):
        rows = slice(128 * n, 128 * n + 128)
        t = dot(m2h[rows, :], bz[0]) + dot(m2l[rows, :], bz[0]) + dot(m2h[rows, :], bz[1])
        hi, lo = split(t * kt[rows, :])
        m3h[rows, :] = hi
        m3l[rows, :] = lo

    relay(MIDDLE)

    for n in range(8):
        rows = slice(64 * n, 64 * n + 64)
        for h in range(2):
            cols = slice(256 * h, 256 * h + 256)
            w = dot(m3h[rows, cols], bzi[...])
            t = w[:, 0:128] + w[:, 128:256] + dot(m3l[rows, cols], bzi[:, 0:128])
            hi, lo = split(t)
            out = pl.ds((2 * n + h) * 128, 128)
            m4[0:64, out] = hi
            m4[64:128, out] = lo
            m4[128:192, out] = hi

    for n in range(8):
        cols = slice(256 * n, 256 * n + 256)
        m5[:, cols] = dot(lyi[...], m4[:, cols])

    sums = []
    for part in range(2):
        vals = []
        for a in range(8):
            cols = slice((8 * part + a) * 128, (8 * part + a) * 128 + 128)
            vals += swap_chunks([m5[8 * j:8 * j + 8, cols] for j in range(4)], odd1, odd2)
        sums.append(combine(trig[32 * part:32 * part + 32, 16:32].T, vals))
    for n in range(16):
        for x, val in ((16 + n, sums[0][n] + sums[1][n]), (15 - n, sums[0][n] - sums[1][n])):
            pbuf[pl.ds(16 * (x // 2) + x % 2, 8, stride=2), :] = val

    slot = (1 - half) * 16 + r

    for vec, h, m in others():
        rows = pl.multiple_of(16 * m + 8 * h, 8)
        pltpu.make_async_remote_copy(
            pbuf.at[pl.ds(rows, 8)], pl_in.at[slot], a2_send, a2_recv,
            device_id=(vec, m), device_id_type=MESH,
        ).start()
    keep = pltpu.make_async_copy(
        pbuf.at[pl.ds(pl.multiple_of(16 * r + 8 * half, 8), 8)], pl_in.at[slot], a2_loc
    )
    keep.start()

    def prepare(d):
        for rho in range(8):
            hi, lo = split(vl[32 * d:32 * d + 32, rho, :])
            vh[32 * d:32 * d + 32, 128 * rho:128 * rho + 128] = hi
            vlo[32 * d:32 * d + 32, 128 * rho:128 * rho + 128] = lo

    pl.when(plane == 1)(relay_up)
    relay(24 - BEFORE - MIDDLE)
    own.wait()
    for k in range(PIECES):
        wait_block(0, 1, k)
    for d in range(REACH):
        prepare(d)
    for k in range(PIECES):
        wait_block(REACH, 0, k)
        wait_block(REACH, 1, k)
    prepare(REACH)

    keep.wait()
    rest = pl_in.at[pl.ds(0, 31)]
    pltpu.make_async_copy(rest, rest, a2_recv).wait()
    parts = [split(pl_in[:, rho, :]) for rho in range(8)]
    ph = jnp.concatenate([p[0] for p in parts], axis=1)
    plo = jnp.concatenate([p[1] for p in parts], axis=1)
    gram = dot_nt(ph, vh[...]) + dot_nt(plo, vh[...]) + dot_nt(ph, vlo[...])
    pad = jnp.zeros((16, 112), F32)
    sb[0:16, 0, :] = gram[0:16, 0:128]
    sb[0:16, 1, :] = jnp.concatenate([gram[0:16, 128:144], pad], axis=1)
    sb[16:32, 0, :] = gram[16:32, 16:144]
    sb[16:32, 1, :] = jnp.concatenate([gram[16:32, 144:160], pad], axis=1)

    for vec, h, m in others():
        pltpu.make_async_remote_copy(
            sb.at[16 * h + m], rl.at[me], r_send, r_recv, device_id=(vec, m), device_id_type=MESH
        ).start()
    keep = pltpu.make_async_copy(sb.at[me], rl.at[me], r_loc)
    keep.start()
    keep.wait()
    rest = rl.at[pl.ds(0, 31)]
    pltpu.make_async_copy(rest, rest, r_recv).wait()
    for c in first:
        c.wait_send()

    @pl.when(straight)
    def _():
        for c in direct:
            c.wait_send()

    @pl.when(upward)
    def _():
        for piece in pieces:
            pass_up(*piece).wait_send()

    @pl.when(middle)
    def _():
        for piece in pieces:
            pass_on(*piece).wait_send()

    for d in range(1, REACH):
        for far in range(2):
            for k in range(PIECES):
                if d < REACH - 1:
                    onward(d, far, k).wait_send()
                else:
                    pl.when(passes)(onward(d, far, k).wait_send)
    pltpu.make_async_copy(u, u, a1_send).wait()
    rest = pl_in.at[pl.ds(0, 31)]
    pltpu.make_async_copy(rest, rest, a2_send).wait()
    rest = rl.at[pl.ds(0, 31)]
    pltpu.make_async_copy(rest, rest, r_send).wait()


def finish(parts, out):
    total = jnp.sum(parts[...], axis=0)
    for s in range(9):
        out[s] = total[s // 8:s // 8 + 1, 16 * (s % 8):16 * (s % 8) + 16]


def body(fitting_vectors):
    ly, lyi, bz, bzi, kt, trig = constants()
    rows = fitting_vectors.reshape(16, 2, 8, 128).transpose(0, 2, 1, 3).reshape(16, 16, 128)
    any_spec = pl.BlockSpec(memory_space=pl.ANY)
    dma = pltpu.SemaphoreType.DMA
    partial = pl.pallas_call(
        functools.partial(body_kernel, trig),
        name="coulomb",
        out_shape=jax.ShapeDtypeStruct((32, 2, 128), F32),
        in_specs=[any_spec] * 6,
        out_specs=any_spec,
        scratch_shapes=[
            pltpu.VMEM((256, 128), F32),
            pltpu.VMEM((256, 128), F32),
            pltpu.VMEM((32, 8, 128), F32),
            pltpu.VMEM((160, 8, 128), F32),
            pltpu.VMEM((32, 8, 128), F32),
            pltpu.VMEM(ly.shape, BF16),
            pltpu.VMEM(lyi.shape, BF16),
            pltpu.VMEM(bz.shape, BF16),
            pltpu.VMEM(bzi.shape, BF16),
            pltpu.VMEM(kt.shape, F32),
            pltpu.VMEM((96, 2048), BF16),
            pltpu.VMEM((512, 256), BF16),
            pltpu.VMEM((512, 256), BF16),
            pltpu.VMEM((512, 512), BF16),
            pltpu.VMEM((512, 512), BF16),
            pltpu.VMEM((192, 2048), BF16),
            pltpu.VMEM((32, 2048), F32),
            pltpu.VMEM((160, 1024), BF16),
            pltpu.VMEM((160, 1024), BF16),
            pltpu.VMEM((32, 2, 128), F32),
            pltpu.SemaphoreType.REGULAR,
            pltpu.SemaphoreType.REGULAR,
            dma((5,)),
            dma, dma,
            dma((14 * PIECES,)), dma((12 * PIECES,)), dma,
            dma, dma, dma,
            dma, dma, dma,
        ],
        compiler_params=pltpu.CompilerParams(collective_id=0, has_side_effects=True),
    )(rows, ly, lyi, bz, bzi, kt)
    out = pl.pallas_call(
        finish,
        name="finish",
        out_shape=jax.ShapeDtypeStruct((9, 1, 16), F32),
        in_specs=[pl.BlockSpec(memory_space=pltpu.VMEM)],
        out_specs=pl.BlockSpec(memory_space=pltpu.VMEM),
    )(partial)
    return out.transpose(1, 0, 2)


def solution(mesh):
    return jax.shard_map(
        body,
        mesh=mesh,
        in_specs=(P("vec", "grid", None),),
        out_specs=P(("vec", "grid"), None, None),
        check_vma=False,
    )
```

```python
import functools
import math

import jax
import jax.numpy as jnp
import numpy as np
from jax import lax
from jax.experimental import pallas as pl
from jax.experimental.pallas import tpu as pltpu
from jax.sharding import PartitionSpec as P

N = 32
PAD = 2 * N
F32 = jnp.float32
BF16 = jnp.bfloat16
MESH = pl.DeviceIdType.MESH
REACH = 4
PIECES = 2
STEP = 16 // PIECES
BEFORE = 12
MIDDLE = 4


def tables():
    pos = np.arange(N) - (N - 1) / 2.0
    freqs = np.concatenate([np.arange(N), np.arange(1, N + 1)])
    phase = 2.0 * np.pi * freqs[:, None] * pos[None, :] / PAD
    trig = np.where(np.arange(PAD)[:, None] < N, np.cos(phase), np.sin(phase))
    weight = np.where((freqs == 0) | (freqs == N), 1.0, 2.0)
    f = freqs.astype(np.float64)
    total = f[:, None, None] ** 2 + f[None, :, None] ** 2 + f[None, None, :] ** 2
    g2 = total * (2.0 * np.pi / PAD) ** 2
    safe = np.where(total > 0, g2, 1.0)
    kernel = 8.0 * np.pi * np.sin(np.sqrt(safe) * (N / 2)) ** 2 / safe
    kernel = np.where(total > 0, kernel, 2.0 * np.pi * N * N)
    kernel = kernel * weight[:, None, None] * weight[None, :, None] * weight[None, None, :]
    kernel = kernel / float(PAD) ** 3 / float(N) ** 3
    return trig, kernel


def split_np(a):
    hi = a.astype(np.float32).astype(BF16)
    lo = (a - hi.astype(np.float64)).astype(np.float32).astype(BF16)
    return hi, lo


def constants():
    trig, kernel = tables()
    row = np.arange(N)
    y_of_row = 4 * (row % 8) + row // 8
    ty = trig[:, y_of_row]
    hi, lo = split_np(ty)
    ly = np.concatenate([hi, hi, lo], axis=1)
    hi, lo = split_np(ty.T)
    lyi = np.concatenate([hi, hi, lo], axis=1)
    hi, lo = split_np(np.kron(np.eye(8), trig.T))
    bz = np.stack([hi, lo])
    hi, lo = split_np(np.kron(np.eye(4), trig))
    bzi = np.concatenate([hi, lo], axis=1)
    kt = kernel.reshape(8, 8, PAD, PAD).transpose(0, 2, 1, 3).reshape(8 * PAD, 8 * PAD)
    return ly, lyi, bz, bzi, kt.astype(np.float32), trig


def split(x):
    hi = x.astype(BF16)
    lo = (x - hi.astype(F32)).astype(BF16)
    return hi, lo


def dot(a, b):
    return jnp.dot(a, b, preferred_element_type=F32)


def dot_nt(a, b):
    return lax.dot_general(a, b, (((1,), (1,)), ((), ())), preferred_element_type=F32)


def combine(matrix, values):
    out = []
    for weights in matrix:
        acc = None
        for w, v in zip(weights, values):
            term = v * np.float32(w)
            acc = term if acc is None else acc + term
        out.append(acc)
    return out


def swap_chunks(tiles, odd1, odd2):
    t0, t1, t2, t3 = tiles

    def pair(a, b, mask, up, down):
        return (
            jnp.where(mask, pltpu.roll(b, up, 1), a),
            jnp.where(mask, b, pltpu.roll(a, down, 1)),
        )

    a0, a1 = pair(t0, t1, odd1, 32, 96)
    a2, a3 = pair(t2, t3, odd1, 32, 96)
    b0, b2 = pair(a0, a2, odd2, 64, 64)
    b1, b3 = pair(a1, a3, odd2, 64, 64)
    return b0, b1, b2, b3


def body_kernel(
    trig,
    v_in, ly_in, lyi_in, bz_in, bzi_in, kt_in,
    rl,
    u, pbuf, pl_in, vl, vp, ly, lyi, bz, bzi, kt,
    m1, m2h, m2l, m3h, m3l, m4, m5, vh, vlo, sb,
    ready, ready_up, c_sem, a1_send, a1_recv, v_send, v_recv, v_loc, a2_send, a2_recv, a2_loc, r_send, r_recv, r_loc,
):
    g = lax.axis_index("vec")
    r = lax.axis_index("grid")
    half = lax.rem(g, 2)
    sib = g + 1 - 2 * half
    down = lax.rem(g + 14, 16)
    down_sib = lax.rem(sib + 14, 16)
    up = lax.rem(g + 2, 16)
    up_sib = lax.rem(sib + 2, 16)

    me = 16 * half + r

    def turn(i):
        return lax.rem(r + i, 16)

    def others():
        for i in range(16):
            yield sib, 1 - half, turn(i)
            if i:
                yield g, half, turn(i)

    plane = g // 2
    barrier = pltpu.get_barrier_semaphore()

    def rank(x, y_hi, parity):
        return 2 * (jnp.minimum(x, 2) + jnp.minimum(2 * y_hi + parity, 2)) + parity

    my_rank = rank(r // 4, lax.rem(r, 4) // 2, half)
    later = [
        (m, (rank(m // 4, m % 4 // 2, 1 - half) > my_rank).astype(jnp.int32))
        for m in range(0, 16, 2)
    ]
    n_later = 2 * functools.reduce(lambda a, b: a + b, [after for _, after in later])

    def greet(sem, vec, to):
        pl.semaphore_signal(sem, inc=1, device_id=(vec, to), device_id_type=MESH)

    greet(barrier, g, r + 1 - 2 * lax.rem(r, 2))

    @pl.when(plane < 7)
    def _():
        greet(barrier, up, r)
        greet(barrier, up_sib, r)

    for m, after in later:
        @pl.when(after == 1)
        def _():
            greet(barrier, sib, m)
            greet(barrier, sib, m + 1)

    @pl.when(plane == 0)
    def _():
        for away in (8, 14):
            greet(barrier, g + away, r)
            greet(barrier, sib + away, r)

    @pl.when(plane == 1)
    def _():
        for away in (4, 12):
            greet(barrier, g + away, r)
            greet(barrier, sib + away, r)

    @pl.when(plane == 2)
    def _():
        greet(barrier, g + 8, r)
        greet(barrier, sib + 8, r)

    @pl.when(plane == 7)
    def _():
        greet(barrier, g - 4, r)
        greet(barrier, sib - 4, r)

    consts = [
        pltpu.make_async_copy(a, b, c_sem.at[i])
        for i, (a, b) in enumerate([(ly_in, ly), (lyi_in, lyi), (bz_in, bz), (bzi_in, bzi), (kt_in, kt)])
    ]
    for c in consts:
        c.start()
    own = pltpu.make_async_copy(
        v_in.at[:, pl.ds(pl.multiple_of(8 * half, 8), 8), :], vl.at[pl.ds(16 * half, 16)], v_loc
    )
    own.start()

    across = jnp.where(plane > 0, 2, 0) + jnp.where(plane > 2, 2, 0) + jnp.where(plane == 7, 2, 0)
    pl.semaphore_wait(barrier, 17 - n_later + across)

    for m, after in later:
        @pl.when(after == 0)
        def _():
            greet(ready, sib, m)
            greet(ready, sib, m + 1)

    @pl.when(plane == 7)
    def _():
        greet(ready_up, up, r)
        greet(ready_up, up_sib, r)

    @pl.when(plane == 3)
    def _():
        greet(ready_up, g - 4, r)
        greet(ready_up, sib - 4, r)

    def block(d, part, k):
        return vl.at[pl.ds(pl.multiple_of(32 * d + 16 * part + STEP * k, STEP), STEP)]

    def sem_of(d, far, k):
        return (2 * d + far) * PIECES + k

    def move(src, d, far, part, k, target, leave=0):
        return pltpu.make_async_remote_copy(
            src, block(d, part, k), v_send.at[sem_of(d + leave, far, k)], v_recv.at[sem_of(d, far, k)],
            device_id=(target, r), device_id_type=MESH,
        )

    def source(h, k):
        return v_in.at[pl.ds(STEP * k, STEP), pl.ds(pl.multiple_of(8 * h, 8), 8), :]

    first = []
    for k in range(PIECES):
        first.append(move(source(half, k), 1, 0, half, k, down))
        first.append(move(source(1 - half, k), 1, 1, half, k, down_sib))
    first += [move(source(1 - half, k), 0, 1, half, k, sib) for k in range(PIECES)]
    passes = jnp.logical_or(plane == 0, plane > 4)
    direct = []
    for k in range(PIECES):
        direct.append(move(source(half, k), REACH, 0, half, k, lax.rem(g + 8, 16), 1))
        direct.append(move(source(1 - half, k), REACH, 1, half, k, lax.rem(sib + 8, 16), 1))

    def pass_block(part, k):
        return vp.at[pl.ds(pl.multiple_of(16 * part + STEP * k, STEP), STEP)]

    def pass_up(far, k):
        vec = lax.rem((sib if far else g) + 4, 16)
        return pltpu.make_async_remote_copy(
            source(1 - half if far else half, k), pass_block(half, k),
            v_send.at[sem_of(REACH + 1, far, k)], v_recv.at[sem_of(REACH + 1, far, k)],
            device_id=(vec, r), device_id_type=MESH,
        )

    def pass_on(far, k):
        part = 1 - half if far else half
        return move(pass_block(part, k), REACH, far, part, k, lax.rem(g + 4, 16), 2)

    pieces = [(far, k) for k in range(PIECES) for far in range(2)]
    straight = jnp.logical_or(plane == 4, plane == 6)
    upward = jnp.logical_or(plane == 5, plane == 7)
    middle = jnp.logical_or(plane == 7, plane == 1)

    def relay_up():
        for far, k in pieces:
            ref = pass_block(1 - half if far else half, k)
            pltpu.make_async_copy(ref, ref, v_recv.at[sem_of(REACH + 1, far, k)]).wait()
            pass_on(far, k).start()

    def start_down():
        for c in first[:2 * PIECES]:
            c.start()

    pl.when(plane > 0)(start_down)

    @pl.when(straight)
    def _():
        for c in direct:
            c.start()

    @pl.when(upward)
    def _():
        for piece in pieces:
            pass_up(*piece).start()

    pl.when(n_later > 0)(lambda: pl.semaphore_wait(ready, n_later))

    for i in range(16):
        m = turn(i)
        pltpu.make_async_remote_copy(
            v_in.at[m], u.at[pl.ds(pl.multiple_of(16 * r, 16), 16)], a1_send, a1_recv,
            device_id=(sib, m), device_id_type=MESH,
        ).start()


    @pl.when(plane == 0)
    def _():
        pl.semaphore_wait(ready_up, 2)
        start_down()

    @pl.when(plane == 1)
    def _():
        pl.semaphore_wait(ready_up, 2)

    def part_of(far):
        return 1 - half if far else half

    def wait_block(d, far, k):
        ref = block(d, part_of(far), k)
        pltpu.make_async_copy(ref, ref, v_recv.at[sem_of(d, far, k)]).wait()

    def onward(d, far, k):
        return move(block(d, part_of(far), k), d + 1, far, part_of(far), k, down)

    hops = iter([(d, far, k) for d in range(1, REACH) for k in range(PIECES) for far in range(2)])

    def relay(count):
        for _ in range(count * 2 * PIECES // 8):
            hop = next(hops)
            wait_block(*hop)
            if hop[0] < REACH - 1:
                onward(*hop).start()
            else:
                pl.when(passes)(onward(*hop).start)

    relay(BEFORE)
    pl.when(plane == 7)(relay_up)
    for c in consts:
        c.wait()
    pltpu.make_async_copy(u, u, a1_recv).wait()
    for c in first[2 * PIECES:]:
        c.start()

    lane = lax.broadcasted_iota(jnp.int32, (8, 128), 1) // 32
    odd1 = lane % 2 == 1
    odd2 = lane >= 2

    def slice_at(x):
        return u[pl.ds(16 * (x // 2) + x % 2, 8, stride=2), :]

    low = [slice_at(15 - n) for n in range(16)]
    high = [slice_at(16 + n) for n in range(16)]
    for part in range(2):
        if part == 0:
            vals = [a + b for a, b in zip(high, low)]
        else:
            vals = [a - b for a, b in zip(high, low)]
        for a in range(8):
            q = 32 * part + 4 * a
            tiles = combine(trig[q:q + 4, 16:32], vals)
            tile = jnp.concatenate(swap_chunks(tiles, odd1, odd2), axis=0)
            hi, lo = split(tile)
            cols = pl.ds((8 * part + a) * 128, 128)
            m1[0:32, cols] = hi
            m1[32:64, cols] = lo
            m1[64:96, cols] = hi

    for n in range(8):
        hi, lo = split(dot(ly[...], m1[:, 256 * n:256 * n + 256]))
        m2h[64 * n:64 * n + 64, :] = hi
        m2l[64 * n:64 * n + 64, :] = lo

    for n in range(4):
        rows = slice(128 * n, 128 * n + 128)
        t = dot(m2h[rows, :], bz[0]) + dot(m2l[rows, :], bz[0]) + dot(m2h[rows, :], bz[1])
        hi, lo = split(t * kt[rows, :])
        m3h[rows, :] = hi
        m3l[rows, :] = lo

    relay(MIDDLE)

    for n in range(8):
        rows = slice(64 * n, 64 * n + 64)
        for h in range(2):
            cols = slice(256 * h, 256 * h + 256)
            w = dot(m3h[rows, cols], bzi[...])
            t = w[:, 0:128] + w[:, 128:256] + dot(m3l[rows, cols], bzi[:, 0:128])
            hi, lo = split(t)
            out = pl.ds((2 * n + h) * 128, 128)
            m4[0:64, out] = hi
            m4[64:128, out] = lo
            m4[128:192, out] = hi

    for n in range(8):
        cols = slice(256 * n, 256 * n + 256)
        m5[:, cols] = dot(lyi[...], m4[:, cols])

    sums = []
    for part in range(2):
        vals = []
        for a in range(8):
            cols = slice((8 * part + a) * 128, (8 * part + a) * 128 + 128)
            vals += swap_chunks([m5[8 * j:8 * j + 8, cols] for j in range(4)], odd1, odd2)
        sums.append(combine(trig[32 * part:32 * part + 32, 16:32].T, vals))
    for n in range(16):
        for x, val in ((16 + n, sums[0][n] + sums[1][n]), (15 - n, sums[0][n] - sums[1][n])):
            pbuf[pl.ds(16 * (x // 2) + x % 2, 8, stride=2), :] = val

    slot = (1 - half) * 16 + r

    for vec, h, m in others():
        rows = pl.multiple_of(16 * m + 8 * h, 8)
        pltpu.make_async_remote_copy(
            pbuf.at[pl.ds(rows, 8)], pl_in.at[slot], a2_send, a2_recv,
            device_id=(vec, m), device_id_type=MESH,
        ).start()
    keep = pltpu.make_async_copy(
        pbuf.at[pl.ds(pl.multiple_of(16 * r + 8 * half, 8), 8)], pl_in.at[slot], a2_loc
    )
    keep.start()

    def prepare(d):
        for rho in range(8):
            hi, lo = split(vl[32 * d:32 * d + 32, rho, :])
            vh[32 * d:32 * d + 32, 128 * rho:128 * rho + 128] = hi
            vlo[32 * d:32 * d + 32, 128 * rho:128 * rho + 128] = lo

    pl.when(plane == 1)(relay_up)
    relay(24 - BEFORE - MIDDLE)
    own.wait()
    for k in range(PIECES):
        wait_block(0, 1, k)
    for d in range(REACH):
        prepare(d)
    keep.wait()
    rest = pl_in.at[pl.ds(0, 31)]
    pltpu.make_async_copy(rest, rest, a2_recv).wait()
    parts = [split(pl_in[:, rho, :]) for rho in range(8)]
    ph = jnp.concatenate([p[0] for p in parts], axis=1)
    plo = jnp.concatenate([p[1] for p in parts], axis=1)

    def gram(rows):
        return dot_nt(ph, vh[rows, :]) + dot_nt(plo, vh[rows, :]) + dot_nt(ph, vlo[rows, :])

    near = gram(slice(0, 32 * REACH))
    sb[0:16, 0, :] = near[0:16, :]
    for k in range(PIECES):
        wait_block(REACH, 0, k)
        wait_block(REACH, 1, k)
    prepare(REACH)
    last = gram(slice(32 * REACH, 32 * REACH + 32))
    pad = jnp.zeros((16, 112), F32)
    sb[0:16, 1, :] = jnp.concatenate([last[0:16, 0:16], pad], axis=1)
    sb[16:32, 0, :] = jnp.concatenate([near[16:32, 16:128], last[16:32, 0:16]], axis=1)
    sb[16:32, 1, :] = jnp.concatenate([last[16:32, 16:32], pad], axis=1)

    for vec, h, m in others():
        pltpu.make_async_remote_copy(
            sb.at[16 * h + m], rl.at[me], r_send, r_recv, device_id=(vec, m), device_id_type=MESH
        ).start()
    keep = pltpu.make_async_copy(sb.at[me], rl.at[me], r_loc)
    keep.start()
    keep.wait()
    rest = rl.at[pl.ds(0, 31)]
    pltpu.make_async_copy(rest, rest, r_recv).wait()
    for c in first:
        c.wait_send()

    @pl.when(straight)
    def _():
        for c in direct:
            c.wait_send()

    @pl.when(upward)
    def _():
        for piece in pieces:
            pass_up(*piece).wait_send()

    @pl.when(middle)
    def _():
        for piece in pieces:
            pass_on(*piece).wait_send()

    for d in range(1, REACH):
        for far in range(2):
            for k in range(PIECES):
                if d < REACH - 1:
                    onward(d, far, k).wait_send()
                else:
                    pl.when(passes)(onward(d, far, k).wait_send)
    pltpu.make_async_copy(u, u, a1_send).wait()
    rest = pl_in.at[pl.ds(0, 31)]
    pltpu.make_async_copy(rest, rest, a2_send).wait()
    rest = rl.at[pl.ds(0, 31)]
    pltpu.make_async_copy(rest, rest, r_send).wait()


def finish(parts, out):
    total = jnp.sum(parts[...], axis=0)
    for s in range(9):
        out[s] = total[s // 8:s // 8 + 1, 16 * (s % 8):16 * (s % 8) + 16]


def body(fitting_vectors):
    ly, lyi, bz, bzi, kt, trig = constants()
    rows = fitting_vectors.reshape(16, 2, 8, 128).transpose(0, 2, 1, 3).reshape(16, 16, 128)
    any_spec = pl.BlockSpec(memory_space=pl.ANY)
    dma = pltpu.SemaphoreType.DMA
    partial = pl.pallas_call(
        functools.partial(body_kernel, trig),
        name="coulomb",
        out_shape=jax.ShapeDtypeStruct((32, 2, 128), F32),
        in_specs=[any_spec] * 6,
        out_specs=any_spec,
        scratch_shapes=[
            pltpu.VMEM((256, 128), F32),
            pltpu.VMEM((256, 128), F32),
            pltpu.VMEM((32, 8, 128), F32),
            pltpu.VMEM((160, 8, 128), F32),
            pltpu.VMEM((32, 8, 128), F32),
            pltpu.VMEM(ly.shape, BF16),
            pltpu.VMEM(lyi.shape, BF16),
            pltpu.VMEM(bz.shape, BF16),
            pltpu.VMEM(bzi.shape, BF16),
            pltpu.VMEM(kt.shape, F32),
            pltpu.VMEM((96, 2048), BF16),
            pltpu.VMEM((512, 256), BF16),
            pltpu.VMEM((512, 256), BF16),
            pltpu.VMEM((512, 512), BF16),
            pltpu.VMEM((512, 512), BF16),
            pltpu.VMEM((192, 2048), BF16),
            pltpu.VMEM((32, 2048), F32),
            pltpu.VMEM((160, 1024), BF16),
            pltpu.VMEM((160, 1024), BF16),
            pltpu.VMEM((32, 2, 128), F32),
            pltpu.SemaphoreType.REGULAR,
            pltpu.SemaphoreType.REGULAR,
            dma((5,)),
            dma, dma,
            dma((14 * PIECES,)), dma((12 * PIECES,)), dma,
            dma, dma, dma,
            dma, dma, dma,
        ],
        compiler_params=pltpu.CompilerParams(collective_id=0, has_side_effects=True),
    )(rows, ly, lyi, bz, bzi, kt)
    out = pl.pallas_call(
        finish,
        name="finish",
        out_shape=jax.ShapeDtypeStruct((9, 1, 16), F32),
        in_specs=[pl.BlockSpec(memory_space=pltpu.VMEM)],
        out_specs=pl.BlockSpec(memory_space=pltpu.VMEM),
    )(partial)
    return out.transpose(1, 0, 2)


def solution(mesh):
    return jax.shard_map(
        body,
        mesh=mesh,
        in_specs=(P("vec", "grid", None),),
        out_specs=P(("vec", "grid"), None, None),
        check_vma=False,
    )
```

```python
import functools
import math

import jax
import jax.numpy as jnp
import numpy as np
from jax import lax
from jax.experimental import pallas as pl
from jax.experimental.pallas import tpu as pltpu
from jax.sharding import PartitionSpec as P

N = 32
PAD = 2 * N
F32 = jnp.float32
BF16 = jnp.bfloat16
MESH = pl.DeviceIdType.MESH
REACH = 4
PIECES = 2
STEP = 16 // PIECES
BEFORE = 12
MIDDLE = 4


def tables():
    pos = np.arange(N) - (N - 1) / 2.0
    freqs = np.concatenate([np.arange(N), np.arange(1, N + 1)])
    phase = 2.0 * np.pi * freqs[:, None] * pos[None, :] / PAD
    trig = np.where(np.arange(PAD)[:, None] < N, np.cos(phase), np.sin(phase))
    weight = np.where((freqs == 0) | (freqs == N), 1.0, 2.0)
    f = freqs.astype(np.float64)
    total = f[:, None, None] ** 2 + f[None, :, None] ** 2 + f[None, None, :] ** 2
    g2 = total * (2.0 * np.pi / PAD) ** 2
    safe = np.where(total > 0, g2, 1.0)
    kernel = 8.0 * np.pi * np.sin(np.sqrt(safe) * (N / 2)) ** 2 / safe
    kernel = np.where(total > 0, kernel, 2.0 * np.pi * N * N)
    kernel = kernel * weight[:, None, None] * weight[None, :, None] * weight[None, None, :]
    kernel = kernel / float(PAD) ** 3 / float(N) ** 3
    return trig, kernel


def split_np(a):
    hi = a.astype(np.float32).astype(BF16)
    lo = (a - hi.astype(np.float64)).astype(np.float32).astype(BF16)
    return hi, lo


def constants():
    trig, kernel = tables()
    row = np.arange(N)
    y_of_row = 4 * (row % 8) + row // 8
    ty = trig[:, y_of_row]
    hi, lo = split_np(ty)
    ly = np.concatenate([hi, hi, lo], axis=1)
    hi, lo = split_np(ty.T)
    lyi = np.concatenate([hi, hi, lo], axis=1)
    hi, lo = split_np(np.kron(np.eye(8), trig.T))
    bz = np.stack([hi, lo])
    hi, lo = split_np(np.kron(np.eye(4), trig))
    bzi = np.concatenate([hi, lo], axis=1)
    kt = kernel.reshape(8, 8, PAD, PAD).transpose(0, 2, 1, 3).reshape(8 * PAD, 8 * PAD)
    return ly, lyi, bz, bzi, kt.astype(np.float32), trig


def split(x):
    hi = x.astype(BF16)
    lo = (x - hi.astype(F32)).astype(BF16)
    return hi, lo


def dot(a, b):
    return jnp.dot(a, b, preferred_element_type=F32)


def dot_nt(a, b):
    return lax.dot_general(a, b, (((1,), (1,)), ((), ())), preferred_element_type=F32)


def combine(matrix, values):
    out = []
    for weights in matrix:
        acc = None
        for w, v in zip(weights, values):
            term = v * np.float32(w)
            acc = term if acc is None else acc + term
        out.append(acc)
    return out


def swap_chunks(tiles, odd1, odd2):
    t0, t1, t2, t3 = tiles

    def pair(a, b, mask, up, down):
        return (
            jnp.where(mask, pltpu.roll(b, up, 1), a),
            jnp.where(mask, b, pltpu.roll(a, down, 1)),
        )

    a0, a1 = pair(t0, t1, odd1, 32, 96)
    a2, a3 = pair(t2, t3, odd1, 32, 96)
    b0, b2 = pair(a0, a2, odd2, 64, 64)
    b1, b3 = pair(a1, a3, odd2, 64, 64)
    return b0, b1, b2, b3


def body_kernel(
    trig,
    v_in, ly_in, lyi_in, bz_in, bzi_in, kt_in,
    rl,
    u, pbuf, pl_in, vl, vp, ly, lyi, bz, bzi, kt,
    m1, m2h, m2l, m3h, m3l, m4, m5, vh, vlo, sb,
    ready, ready_up, c_sem, a1_send, a1_recv, v_send, v_recv, v_loc, a2_send, a2_recv, a2_loc, r_send, r_recv, r_loc,
):
    g = lax.axis_index("vec")
    r = lax.axis_index("grid")
    half = lax.rem(g, 2)
    sib = g + 1 - 2 * half
    down = lax.rem(g + 14, 16)
    down_sib = lax.rem(sib + 14, 16)
    up = lax.rem(g + 2, 16)
    up_sib = lax.rem(sib + 2, 16)

    me = 16 * half + r

    def turn(i):
        return lax.rem(r + i, 16)

    def others():
        for i in range(16):
            yield sib, 1 - half, turn(i)
            if i:
                yield g, half, turn(i)

    plane = g // 2
    barrier = pltpu.get_barrier_semaphore()

    def rank(x, y_hi, parity):
        return 2 * (jnp.minimum(x, 2) + jnp.minimum(2 * y_hi + parity, 2)) + parity

    my_rank = rank(r // 4, lax.rem(r, 4) // 2, half)
    later = [
        (m, (rank(m // 4, m % 4 // 2, 1 - half) > my_rank).astype(jnp.int32)) for m in range(16)
    ]
    n_later = functools.reduce(lambda a, b: a + b, [after for _, after in later])

    def greet(sem, vec, to):
        pl.semaphore_signal(sem, inc=1, device_id=(vec, to), device_id_type=MESH)

    greet(barrier, g, r + 1 - 2 * lax.rem(r, 2))

    @pl.when(plane < 7)
    def _():
        greet(barrier, up, r)
        greet(barrier, up_sib, r)

    for m, after in later:
        pl.when(after == 1)(functools.partial(greet, barrier, sib, m))

    @pl.when(plane == 0)
    def _():
        for away in (8, 14):
            greet(barrier, g + away, r)
            greet(barrier, sib + away, r)

    @pl.when(plane == 1)
    def _():
        for away in (4, 12):
            greet(barrier, g + away, r)
            greet(barrier, sib + away, r)

    @pl.when(plane == 2)
    def _():
        greet(barrier, g + 8, r)
        greet(barrier, sib + 8, r)

    @pl.when(plane == 7)
    def _():
        greet(barrier, g - 4, r)
        greet(barrier, sib - 4, r)

    consts = [
        pltpu.make_async_copy(a, b, c_sem.at[i])
        for i, (a, b) in enumerate([(ly_in, ly), (lyi_in, lyi), (bz_in, bz), (bzi_in, bzi), (kt_in, kt)])
    ]
    for c in consts:
        c.start()
    own = pltpu.make_async_copy(
        v_in.at[:, pl.ds(pl.multiple_of(8 * half, 8), 8), :], vl.at[pl.ds(16 * half, 16)], v_loc
    )
    own.start()

    across = jnp.where(plane > 0, 2, 0) + jnp.where(plane > 2, 2, 0) + jnp.where(plane == 7, 2, 0)
    pl.semaphore_wait(barrier, 17 - n_later + across)

    for m, after in later:
        pl.when(after == 0)(functools.partial(greet, ready, sib, m))

    @pl.when(plane == 7)
    def _():
        greet(ready_up, up, r)
        greet(ready_up, up_sib, r)

    @pl.when(plane == 3)
    def _():
        greet(ready_up, g - 4, r)
        greet(ready_up, sib - 4, r)

    def block(d, part, k):
        return vl.at[pl.ds(pl.multiple_of(32 * d + 16 * part + STEP * k, STEP), STEP)]

    def sem_of(d, far, k):
        return (2 * d + far) * PIECES + k

    def move(src, d, far, part, k, target, leave=0):
        return pltpu.make_async_remote_copy(
            src, block(d, part, k), v_send.at[sem_of(d + leave, far, k)], v_recv.at[sem_of(d, far, k)],
            device_id=(target, r), device_id_type=MESH,
        )

    def source(h, k):
        return v_in.at[pl.ds(STEP * k, STEP), pl.ds(pl.multiple_of(8 * h, 8), 8), :]

    first = []
    for k in range(PIECES):
        first.append(move(source(half, k), 1, 0, half, k, down))
        first.append(move(source(1 - half, k), 1, 1, half, k, down_sib))
    first += [move(source(1 - half, k), 0, 1, half, k, sib) for k in range(PIECES)]
    passes = jnp.logical_or(plane == 0, plane > 4)
    direct = []
    for k in range(PIECES):
        direct.append(move(source(half, k), REACH, 0, half, k, lax.rem(g + 8, 16), 1))
        direct.append(move(source(1 - half, k), REACH, 1, half, k, lax.rem(sib + 8, 16), 1))

    def pass_block(part, k):
        return vp.at[pl.ds(pl.multiple_of(16 * part + STEP * k, STEP), STEP)]

    def pass_up(far, k):
        vec = lax.rem((sib if far else g) + 4, 16)
        return pltpu.make_async_remote_copy(
            source(1 - half if far else half, k), pass_block(half, k),
            v_send.at[sem_of(REACH + 1, far, k)], v_recv.at[sem_of(REACH + 1, far, k)],
            device_id=(vec, r), device_id_type=MESH,
        )

    def pass_on(far, k):
        part = 1 - half if far else half
        return move(pass_block(part, k), REACH, far, part, k, lax.rem(g + 4, 16), 2)

    pieces = [(far, k) for k in range(PIECES) for far in range(2)]
    straight = jnp.logical_or(plane == 4, plane == 6)
    upward = jnp.logical_or(plane == 5, plane == 7)
    middle = jnp.logical_or(plane == 7, plane == 1)

    def relay_up():
        for far, k in pieces:
            ref = pass_block(1 - half if far else half, k)
            pltpu.make_async_copy(ref, ref, v_recv.at[sem_of(REACH + 1, far, k)]).wait()
            pass_on(far, k).start()

    def start_down():
        for c in first[:2 * PIECES]:
            c.start()

    pl.when(plane > 0)(start_down)

    @pl.when(straight)
    def _():
        for c in direct:
            c.start()

    @pl.when(upward)
    def _():
        for piece in pieces:
            pass_up(*piece).start()

    pl.when(n_later > 0)(lambda: pl.semaphore_wait(ready, n_later))

    for i in range(16):
        m = turn(i)
        pltpu.make_async_remote_copy(
            v_in.at[m], u.at[pl.ds(pl.multiple_of(16 * r, 16), 16)], a1_send, a1_recv,
            device_id=(sib, m), device_id_type=MESH,
        ).start()

    for c in first[2 * PIECES:]:
        c.start()

    @pl.when(plane == 0)
    def _():
        pl.semaphore_wait(ready_up, 2)
        start_down()

    @pl.when(plane == 1)
    def _():
        pl.semaphore_wait(ready_up, 2)

    def part_of(far):
        return 1 - half if far else half

    def wait_block(d, far, k):
        ref = block(d, part_of(far), k)
        pltpu.make_async_copy(ref, ref, v_recv.at[sem_of(d, far, k)]).wait()

    def onward(d, far, k):
        return move(block(d, part_of(far), k), d + 1, far, part_of(far), k, down)

    hops = iter([(d, far, k) for d in range(1, REACH) for k in range(PIECES) for far in range(2)])

    def relay(count):
        for _ in range(count * 2 * PIECES // 8):
            hop = next(hops)
            wait_block(*hop)
            if hop[0] < REACH - 1:
                onward(*hop).start()
            else:
                pl.when(passes)(onward(*hop).start)

    relay(BEFORE)
    pl.when(plane == 7)(relay_up)
    for c in consts:
        c.wait()
    pltpu.make_async_copy(u, u, a1_recv).wait()

    lane = lax.broadcasted_iota(jnp.int32, (8, 128), 1) // 32
    odd1 = lane % 2 == 1
    odd2 = lane >= 2

    def slice_at(x):
        return u[pl.ds(16 * (x // 2) + x % 2, 8, stride=2), :]

    low = [slice_at(15 - n) for n in range(16)]
    high = [slice_at(16 + n) for n in range(16)]
    for part in range(2):
        if part == 0:
            vals = [a + b for a, b in zip(high, low)]
        else:
            vals = [a - b for a, b in zip(high, low)]
        for a in range(8):
            q = 32 * part + 4 * a
            tiles = combine(trig[q:q + 4, 16:32], vals)
            tile = jnp.concatenate(swap_chunks(tiles, odd1, odd2), axis=0)
            hi, lo = split(tile)
            cols = pl.ds((8 * part + a) * 128, 128)
            m1[0:32, cols] = hi
            m1[32:64, cols] = lo
            m1[64:96, cols] = hi

    for n in range(8):
        hi, lo = split(dot(ly[...], m1[:, 256 * n:256 * n + 256]))
        m2h[64 * n:64 * n + 64, :] = hi
        m2l[64 * n:64 * n + 64, :] = lo

    for n in range(4):
        rows = slice(128 * n, 128 * n + 128)
        t = dot(m2h[rows, :], bz[0]) + dot(m2l[rows, :], bz[0]) + dot(m2h[rows, :], bz[1])
        hi, lo = split(t * kt[rows, :])
        m3h[rows, :] = hi
        m3l[rows, :] = lo

    relay(MIDDLE)

    for n in range(8):
        rows = slice(64 * n, 64 * n + 64)
        for h in range(2):
            cols = slice(256 * h, 256 * h + 256)
            w = dot(m3h[rows, cols], bzi[...])
            t = w[:, 0:128] + w[:, 128:256] + dot(m3l[rows, cols], bzi[:, 0:128])
            hi, lo = split(t)
            out = pl.ds((2 * n + h) * 128, 128)
            m4[0:64, out] = hi
            m4[64:128, out] = lo
            m4[128:192, out] = hi

    for n in range(8):
        cols = slice(256 * n, 256 * n + 256)
        m5[:, cols] = dot(lyi[...], m4[:, cols])

    slot = (1 - half) * 16 + r
    slots = []
    for part in range(2):
        vals = []
        for a in range(8):
            cols = slice((8 * part + a) * 128, (8 * part + a) * 128 + 128)
            vals += swap_chunks([m5[8 * j:8 * j + 8, cols] for j in range(4)], odd1, odd2)
        slots.append(vals)

    def send_potential(vec, h, m):
        rows = pl.multiple_of(16 * m + 8 * h, 8)
        pltpu.make_async_remote_copy(
            pbuf.at[pl.ds(rows, 8)], pl_in.at[slot], a2_send, a2_recv,
            device_id=(vec, m), device_id_type=MESH,
        ).start()

    for n in range(16):
        even, odd = [
            combine(trig[32 * part:32 * part + 32, 16 + n:17 + n].T, slots[part])[0] for part in range(2)
        ]
        for x, val in ((16 + n, even + odd), (15 - n, even - odd)):
            pbuf[pl.ds(16 * (x // 2) + x % 2, 8, stride=2), :] = val
        if n % 2:
            for m in (8 + n // 2, 7 - n // 2):
                send_potential(sib, 1 - half, m)
                pl.when(r != m)(functools.partial(send_potential, g, half, m))
    keep = pltpu.make_async_copy(
        pbuf.at[pl.ds(pl.multiple_of(16 * r + 8 * half, 8), 8)], pl_in.at[slot], a2_loc
    )
    keep.start()

    def prepare(d):
        for rho in range(8):
            hi, lo = split(vl[32 * d:32 * d + 32, rho, :])
            vh[32 * d:32 * d + 32, 128 * rho:128 * rho + 128] = hi
            vlo[32 * d:32 * d + 32, 128 * rho:128 * rho + 128] = lo

    pl.when(plane == 1)(relay_up)
    relay(24 - BEFORE - MIDDLE)
    own.wait()
    for k in range(PIECES):
        wait_block(0, 1, k)
    for d in range(REACH):
        prepare(d)
    for k in range(PIECES):
        wait_block(REACH, 0, k)
        wait_block(REACH, 1, k)
    prepare(REACH)

    keep.wait()
    rest = pl_in.at[pl.ds(0, 31)]
    pltpu.make_async_copy(rest, rest, a2_recv).wait()
    parts = [split(pl_in[:, rho, :]) for rho in range(8)]
    ph = jnp.concatenate([p[0] for p in parts], axis=1)
    plo = jnp.concatenate([p[1] for p in parts], axis=1)
    gram = dot_nt(ph, vh[...]) + dot_nt(plo, vh[...]) + dot_nt(ph, vlo[...])
    pad = jnp.zeros((16, 112), F32)
    sb[0:16, 0, :] = gram[0:16, 0:128]
    sb[0:16, 1, :] = jnp.concatenate([gram[0:16, 128:144], pad], axis=1)
    sb[16:32, 0, :] = gram[16:32, 16:144]
    sb[16:32, 1, :] = jnp.concatenate([gram[16:32, 144:160], pad], axis=1)

    for vec, h, m in others():
        pltpu.make_async_remote_copy(
            sb.at[16 * h + m], rl.at[me], r_send, r_recv, device_id=(vec, m), device_id_type=MESH
        ).start()
    keep = pltpu.make_async_copy(sb.at[me], rl.at[me], r_loc)
    keep.start()
    keep.wait()
    rest = rl.at[pl.ds(0, 31)]
    pltpu.make_async_copy(rest, rest, r_recv).wait()
    for c in first:
        c.wait_send()

    @pl.when(straight)
    def _():
        for c in direct:
            c.wait_send()

    @pl.when(upward)
    def _():
        for piece in pieces:
            pass_up(*piece).wait_send()

    @pl.when(middle)
    def _():
        for piece in pieces:
            pass_on(*piece).wait_send()

    for d in range(1, REACH):
        for far in range(2):
            for k in range(PIECES):
                if d < REACH - 1:
                    onward(d, far, k).wait_send()
                else:
                    pl.when(passes)(onward(d, far, k).wait_send)
    pltpu.make_async_copy(u, u, a1_send).wait()
    rest = pl_in.at[pl.ds(0, 31)]
    pltpu.make_async_copy(rest, rest, a2_send).wait()
    rest = rl.at[pl.ds(0, 31)]
    pltpu.make_async_copy(rest, rest, r_send).wait()


def finish(parts, out):
    total = jnp.sum(parts[...], axis=0)
    for s in range(9):
        out[s] = total[s // 8:s // 8 + 1, 16 * (s % 8):16 * (s % 8) + 16]


def body(fitting_vectors):
    ly, lyi, bz, bzi, kt, trig = constants()
    rows = fitting_vectors.reshape(16, 2, 8, 128).transpose(0, 2, 1, 3).reshape(16, 16, 128)
    any_spec = pl.BlockSpec(memory_space=pl.ANY)
    dma = pltpu.SemaphoreType.DMA
    partial = pl.pallas_call(
        functools.partial(body_kernel, trig),
        name="coulomb",
        out_shape=jax.ShapeDtypeStruct((32, 2, 128), F32),
        in_specs=[any_spec] * 6,
        out_specs=any_spec,
        scratch_shapes=[
            pltpu.VMEM((256, 128), F32),
            pltpu.VMEM((256, 128), F32),
            pltpu.VMEM((32, 8, 128), F32),
            pltpu.VMEM((160, 8, 128), F32),
            pltpu.VMEM((32, 8, 128), F32),
            pltpu.VMEM(ly.shape, BF16),
            pltpu.VMEM(lyi.shape, BF16),
            pltpu.VMEM(bz.shape, BF16),
            pltpu.VMEM(bzi.shape, BF16),
            pltpu.VMEM(kt.shape, F32),
            pltpu.VMEM((96, 2048), BF16),
            pltpu.VMEM((512, 256), BF16),
            pltpu.VMEM((512, 256), BF16),
            pltpu.VMEM((512, 512), BF16),
            pltpu.VMEM((512, 512), BF16),
            pltpu.VMEM((192, 2048), BF16),
            pltpu.VMEM((32, 2048), F32),
            pltpu.VMEM((160, 1024), BF16),
            pltpu.VMEM((160, 1024), BF16),
            pltpu.VMEM((32, 2, 128), F32),
            pltpu.SemaphoreType.REGULAR,
            pltpu.SemaphoreType.REGULAR,
            dma((5,)),
            dma, dma,
            dma((14 * PIECES,)), dma((12 * PIECES,)), dma,
            dma, dma, dma,
            dma, dma, dma,
        ],
        compiler_params=pltpu.CompilerParams(collective_id=0, has_side_effects=True),
    )(rows, ly, lyi, bz, bzi, kt)
    out = pl.pallas_call(
        finish,
        name="finish",
        out_shape=jax.ShapeDtypeStruct((9, 1, 16), F32),
        in_specs=[pl.BlockSpec(memory_space=pltpu.VMEM)],
        out_specs=pl.BlockSpec(memory_space=pltpu.VMEM),
    )(partial)
    return out.transpose(1, 0, 2)


def solution(mesh):
    return jax.shard_map(
        body,
        mesh=mesh,
        in_specs=(P("vec", "grid", None),),
        out_specs=P(("vec", "grid"), None, None),
        check_vma=False,
    )
```

```python
import functools
import math

import jax
import jax.numpy as jnp
import numpy as np
from jax import lax
from jax.experimental import pallas as pl
from jax.experimental.pallas import tpu as pltpu
from jax.sharding import PartitionSpec as P

N = 32
PAD = 2 * N
F32 = jnp.float32
BF16 = jnp.bfloat16
MESH = pl.DeviceIdType.MESH
REACH = 4
PIECES = 2
STEP = 16 // PIECES
BEFORE = 10
MIDDLE = 6


def tables():
    pos = np.arange(N) - (N - 1) / 2.0
    freqs = np.concatenate([np.arange(N), np.arange(1, N + 1)])
    phase = 2.0 * np.pi * freqs[:, None] * pos[None, :] / PAD
    trig = np.where(np.arange(PAD)[:, None] < N, np.cos(phase), np.sin(phase))
    weight = np.where((freqs == 0) | (freqs == N), 1.0, 2.0)
    f = freqs.astype(np.float64)
    total = f[:, None, None] ** 2 + f[None, :, None] ** 2 + f[None, None, :] ** 2
    g2 = total * (2.0 * np.pi / PAD) ** 2
    safe = np.where(total > 0, g2, 1.0)
    kernel = 8.0 * np.pi * np.sin(np.sqrt(safe) * (N / 2)) ** 2 / safe
    kernel = np.where(total > 0, kernel, 2.0 * np.pi * N * N)
    kernel = kernel * weight[:, None, None] * weight[None, :, None] * weight[None, None, :]
    kernel = kernel / float(PAD) ** 3 / float(N) ** 3
    return trig, kernel


def split_np(a):
    hi = a.astype(np.float32).astype(BF16)
    lo = (a - hi.astype(np.float64)).astype(np.float32).astype(BF16)
    return hi, lo


def constants():
    trig, kernel = tables()
    row = np.arange(N)
    y_of_row = 4 * (row % 8) + row // 8
    ty = trig[:, y_of_row]
    hi, lo = split_np(ty)
    ly = np.concatenate([hi, hi, lo], axis=1)
    hi, lo = split_np(ty.T)
    lyi = np.concatenate([hi, hi, lo], axis=1)
    hi, lo = split_np(np.kron(np.eye(8), trig.T))
    bz = np.stack([hi, lo])
    hi, lo = split_np(np.kron(np.eye(4), trig))
    bzi = np.concatenate([hi, lo], axis=1)
    kt = kernel.reshape(8, 8, PAD, PAD).transpose(0, 2, 1, 3).reshape(8 * PAD, 8 * PAD)
    return ly, lyi, bz, bzi, kt.astype(np.float32), trig


def split(x):
    hi = x.astype(BF16)
    lo = (x - hi.astype(F32)).astype(BF16)
    return hi, lo


def dot(a, b):
    return jnp.dot(a, b, preferred_element_type=F32)


def dot_nt(a, b):
    return lax.dot_general(a, b, (((1,), (1,)), ((), ())), preferred_element_type=F32)


def combine(matrix, values):
    out = []
    for weights in matrix:
        acc = None
        for w, v in zip(weights, values):
            term = v * np.float32(w)
            acc = term if acc is None else acc + term
        out.append(acc)
    return out


def swap_chunks(tiles, odd1, odd2):
    t0, t1, t2, t3 = tiles

    def pair(a, b, mask, up, down):
        return (
            jnp.where(mask, pltpu.roll(b, up, 1), a),
            jnp.where(mask, b, pltpu.roll(a, down, 1)),
        )

    a0, a1 = pair(t0, t1, odd1, 32, 96)
    a2, a3 = pair(t2, t3, odd1, 32, 96)
    b0, b2 = pair(a0, a2, odd2, 64, 64)
    b1, b3 = pair(a1, a3, odd2, 64, 64)
    return b0, b1, b2, b3


def body_kernel(
    trig,
    v_in, ly_in, lyi_in, bz_in, bzi_in, kt_in,
    rl,
    u, pbuf, pl_in, vl, vp, ly, lyi, bz, bzi, kt,
    m1, m2h, m2l, m3h, m3l, m4, m5, vh, vlo, sb,
    ready, ready_up, c_sem, a1_send, a1_recv, v_send, v_recv, v_loc, a2_send, a2_recv, a2_loc, r_send, r_recv, r_loc,
):
    g = lax.axis_index("vec")
    r = lax.axis_index("grid")
    half = lax.rem(g, 2)
    sib = g + 1 - 2 * half
    down = lax.rem(g + 14, 16)
    down_sib = lax.rem(sib + 14, 16)
    up = lax.rem(g + 2, 16)
    up_sib = lax.rem(sib + 2, 16)

    me = 16 * half + r

    def turn(i):
        return lax.rem(r + i, 16)

    def others():
        for i in range(16):
            yield sib, 1 - half, turn(i)
            if i:
                yield g, half, turn(i)

    plane = g // 2
    barrier = pltpu.get_barrier_semaphore()

    def rank(x, y_hi, parity):
        return 2 * (jnp.minimum(x, 2) + jnp.minimum(2 * y_hi + parity, 2)) + parity

    my_rank = rank(r // 4, lax.rem(r, 4) // 2, half)
    later = [
        (m, (rank(m // 4, m % 4 // 2, 1 - half) > my_rank).astype(jnp.int32)) for m in range(16)
    ]
    n_later = functools.reduce(lambda a, b: a + b, [after for _, after in later])

    def greet(sem, vec, to):
        pl.semaphore_signal(sem, inc=1, device_id=(vec, to), device_id_type=MESH)

    greet(barrier, g, r + 1 - 2 * lax.rem(r, 2))

    @pl.when(plane < 7)
    def _():
        greet(barrier, up, r)
        greet(barrier, up_sib, r)

    for m, after in later:
        pl.when(after == 1)(functools.partial(greet, barrier, sib, m))

    @pl.when(plane == 0)
    def _():
        for away in (8, 14):
            greet(barrier, g + away, r)
            greet(barrier, sib + away, r)

    @pl.when(plane == 1)
    def _():
        for away in (4, 12):
            greet(barrier, g + away, r)
            greet(barrier, sib + away, r)

    @pl.when(plane == 2)
    def _():
        greet(barrier, g + 8, r)
        greet(barrier, sib + 8, r)

    @pl.when(plane == 7)
    def _():
        greet(barrier, g - 4, r)
        greet(barrier, sib - 4, r)

    consts = [
        pltpu.make_async_copy(a, b, c_sem.at[i])
        for i, (a, b) in enumerate([(ly_in, ly), (lyi_in, lyi), (bz_in, bz), (bzi_in, bzi), (kt_in, kt)])
    ]
    for c in consts:
        c.start()
    own = pltpu.make_async_copy(
        v_in.at[:, pl.ds(pl.multiple_of(8 * half, 8), 8), :], vl.at[pl.ds(16 * half, 16)], v_loc
    )
    own.start()

    across = jnp.where(plane > 0, 2, 0) + jnp.where(plane > 2, 2, 0) + jnp.where(plane == 7, 2, 0)
    pl.semaphore_wait(barrier, 17 - n_later + across)

    for m, after in later:
        pl.when(after == 0)(functools.partial(greet, ready, sib, m))

    @pl.when(plane == 7)
    def _():
        greet(ready_up, up, r)
        greet(ready_up, up_sib, r)

    @pl.when(plane == 3)
    def _():
        greet(ready_up, g - 4, r)
        greet(ready_up, sib - 4, r)

    def block(d, part, k):
        return vl.at[pl.ds(pl.multiple_of(32 * d + 16 * part + STEP * k, STEP), STEP)]

    def sem_of(d, far, k):
        return (2 * d + far) * PIECES + k

    def move(src, d, far, part, k, target, leave=0):
        return pltpu.make_async_remote_copy(
            src, block(d, part, k), v_send.at[sem_of(d + leave, far, k)], v_recv.at[sem_of(d, far, k)],
            device_id=(target, r), device_id_type=MESH,
        )

    def source(h, k):
        return v_in.at[pl.ds(STEP * k, STEP), pl.ds(pl.multiple_of(8 * h, 8), 8), :]

    first = []
    for k in range(PIECES):
        first.append(move(source(half, k), 1, 0, half, k, down))
        first.append(move(source(1 - half, k), 1, 1, half, k, down_sib))
    first += [move(source(1 - half, k), 0, 1, half, k, sib) for k in range(PIECES)]
    passes = jnp.logical_or(plane == 0, plane > 4)
    direct = []
    for k in range(PIECES):
        direct.append(move(source(half, k), REACH, 0, half, k, lax.rem(g + 8, 16), 1))
        direct.append(move(source(1 - half, k), REACH, 1, half, k, lax.rem(sib + 8, 16), 1))

    def pass_block(part, k):
        return vp.at[pl.ds(pl.multiple_of(16 * part + STEP * k, STEP), STEP)]

    def pass_up(far, k):
        vec = lax.rem((sib if far else g) + 4, 16)
        return pltpu.make_async_remote_copy(
            source(1 - half if far else half, k), pass_block(half, k),
            v_send.at[sem_of(REACH + 1, far, k)], v_recv.at[sem_of(REACH + 1, far, k)],
            device_id=(vec, r), device_id_type=MESH,
        )

    def pass_on(far, k):
        part = 1 - half if far else half
        return move(pass_block(part, k), REACH, far, part, k, lax.rem(g + 4, 16), 2)

    pieces = [(far, k) for k in range(PIECES) for far in range(2)]
    straight = jnp.logical_or(plane == 4, plane == 6)
    upward = jnp.logical_or(plane == 5, plane == 7)
    middle = jnp.logical_or(plane == 7, plane == 1)

    def relay_up():
        for far, k in pieces:
            ref = pass_block(1 - half if far else half, k)
            pltpu.make_async_copy(ref, ref, v_recv.at[sem_of(REACH + 1, far, k)]).wait()
            pass_on(far, k).start()

    def start_down():
        for c in first[:2 * PIECES]:
            c.start()

    pl.when(plane > 0)(start_down)

    @pl.when(straight)
    def _():
        for c in direct:
            c.start()

    @pl.when(upward)
    def _():
        for piece in pieces:
            pass_up(*piece).start()

    pl.when(n_later > 0)(lambda: pl.semaphore_wait(ready, n_later))

    for i in range(16):
        m = turn(i)
        pltpu.make_async_remote_copy(
            v_in.at[m], u.at[pl.ds(pl.multiple_of(16 * r, 16), 16)], a1_send, a1_recv,
            device_id=(sib, m), device_id_type=MESH,
        ).start()

    for c in first[2 * PIECES:]:
        c.start()

    @pl.when(plane == 0)
    def _():
        pl.semaphore_wait(ready_up, 2)
        start_down()

    @pl.when(plane == 1)
    def _():
        pl.semaphore_wait(ready_up, 2)

    def part_of(far):
        return 1 - half if far else half

    def wait_block(d, far, k):
        ref = block(d, part_of(far), k)
        pltpu.make_async_copy(ref, ref, v_recv.at[sem_of(d, far, k)]).wait()

    def onward(d, far, k):
        return move(block(d, part_of(far), k), d + 1, far, part_of(far), k, down)

    hops = iter([(d, far, k) for d in range(1, REACH) for k in range(PIECES) for far in range(2)])

    def relay(count):
        for _ in range(count * 2 * PIECES // 8):
            hop = next(hops)
            wait_block(*hop)
            if hop[0] < REACH - 1:
                onward(*hop).start()
            else:
                pl.when(passes)(onward(*hop).start)

    relay(BEFORE)
    pl.when(plane == 7)(relay_up)
    for c in consts:
        c.wait()
    pltpu.make_async_copy(u, u, a1_recv).wait()

    lane = lax.broadcasted_iota(jnp.int32, (8, 128), 1) // 32
    odd1 = lane % 2 == 1
    odd2 = lane >= 2

    def slice_at(x):
        return u[pl.ds(16 * (x // 2) + x % 2, 8, stride=2), :]

    low = [slice_at(15 - n) for n in range(16)]
    high = [slice_at(16 + n) for n in range(16)]
    for part in range(2):
        if part == 0:
            vals = [a + b for a, b in zip(high, low)]
        else:
            vals = [a - b for a, b in zip(high, low)]
        for a in range(8):
            q = 32 * part + 4 * a
            tiles = combine(trig[q:q + 4, 16:32], vals)
            tile = jnp.concatenate(swap_chunks(tiles, odd1, odd2), axis=0)
            hi, lo = split(tile)
            cols = pl.ds((8 * part + a) * 128, 128)
            m1[0:32, cols] = hi
            m1[32:64, cols] = lo
            m1[64:96, cols] = hi

    for n in range(8):
        hi, lo = split(dot(ly[...], m1[:, 256 * n:256 * n + 256]))
        m2h[64 * n:64 * n + 64, :] = hi
        m2l[64 * n:64 * n + 64, :] = lo

    for n in range(4):
        rows = slice(128 * n, 128 * n + 128)
        t = dot(m2h[rows, :], bz[0]) + dot(m2l[rows, :], bz[0]) + dot(m2h[rows, :], bz[1])
        hi, lo = split(t * kt[rows, :])
        m3h[rows, :] = hi
        m3l[rows, :] = lo

    relay(MIDDLE)

    for n in range(8):
        rows = slice(64 * n, 64 * n + 64)
        for h in range(2):
            cols = slice(256 * h, 256 * h + 256)
            w = dot(m3h[rows, cols], bzi[...])
            t = w[:, 0:128] + w[:, 128:256] + dot(m3l[rows, cols], bzi[:, 0:128])
            hi, lo = split(t)
            out = pl.ds((2 * n + h) * 128, 128)
            m4[0:64, out] = hi
            m4[64:128, out] = lo
            m4[128:192, out] = hi

    for n in range(8):
        cols = slice(256 * n, 256 * n + 256)
        m5[:, cols] = dot(lyi[...], m4[:, cols])

    sums = []
    for part in range(2):
        vals = []
        for a in range(8):
            cols = slice((8 * part + a) * 128, (8 * part + a) * 128 + 128)
            vals += swap_chunks([m5[8 * j:8 * j + 8, cols] for j in range(4)], odd1, odd2)
        sums.append(combine(trig[32 * part:32 * part + 32, 16:32].T, vals))
    for n in range(16):
        for x, val in ((16 + n, sums[0][n] + sums[1][n]), (15 - n, sums[0][n] - sums[1][n])):
            pbuf[pl.ds(16 * (x // 2) + x % 2, 8, stride=2), :] = val

    slot = (1 - half) * 16 + r

    for vec, h, m in others():
        rows = pl.multiple_of(16 * m + 8 * h, 8)
        pltpu.make_async_remote_copy(
            pbuf.at[pl.ds(rows, 8)], pl_in.at[slot], a2_send, a2_recv,
            device_id=(vec, m), device_id_type=MESH,
        ).start()
    keep = pltpu.make_async_copy(
        pbuf.at[pl.ds(pl.multiple_of(16 * r + 8 * half, 8), 8)], pl_in.at[slot], a2_loc
    )
    keep.start()

    def prepare(d):
        for rho in range(8):
            hi, lo = split(vl[32 * d:32 * d + 32, rho, :])
            vh[32 * d:32 * d + 32, 128 * rho:128 * rho + 128] = hi
            vlo[32 * d:32 * d + 32, 128 * rho:128 * rho + 128] = lo

    pl.when(plane == 1)(relay_up)
    relay(24 - BEFORE - MIDDLE)
    own.wait()
    for k in range(PIECES):
        wait_block(0, 1, k)
    for d in range(REACH):
        prepare(d)
    for k in range(PIECES):
        wait_block(REACH, 0, k)
        wait_block(REACH, 1, k)
    prepare(REACH)

    keep.wait()
    rest = pl_in.at[pl.ds(0, 31)]
    pltpu.make_async_copy(rest, rest, a2_recv).wait()
    parts = [split(pl_in[:, rho, :]) for rho in range(8)]
    ph = jnp.concatenate([p[0] for p in parts], axis=1)
    plo = jnp.concatenate([p[1] for p in parts], axis=1)
    gram = dot_nt(ph, vh[...]) + dot_nt(plo, vh[...]) + dot_nt(ph, vlo[...])
    pad = jnp.zeros((16, 112), F32)
    sb[0:16, 0, :] = gram[0:16, 0:128]
    sb[0:16, 1, :] = jnp.concatenate([gram[0:16, 128:144], pad], axis=1)
    sb[16:32, 0, :] = gram[16:32, 16:144]
    sb[16:32, 1, :] = jnp.concatenate([gram[16:32, 144:160], pad], axis=1)

    for vec, h, m in others():
        pltpu.make_async_remote_copy(
            sb.at[16 * h + m], rl.at[me], r_send, r_recv, device_id=(vec, m), device_id_type=MESH
        ).start()
    keep = pltpu.make_async_copy(sb.at[me], rl.at[me], r_loc)
    keep.start()
    keep.wait()
    rest = rl.at[pl.ds(0, 31)]
    pltpu.make_async_copy(rest, rest, r_recv).wait()
    for c in first:
        c.wait_send()

    @pl.when(straight)
    def _():
        for c in direct:
            c.wait_send()

    @pl.when(upward)
    def _():
        for piece in pieces:
            pass_up(*piece).wait_send()

    @pl.when(middle)
    def _():
        for piece in pieces:
            pass_on(*piece).wait_send()

    for d in range(1, REACH):
        for far in range(2):
            for k in range(PIECES):
                if d < REACH - 1:
                    onward(d, far, k).wait_send()
                else:
                    pl.when(passes)(onward(d, far, k).wait_send)
    pltpu.make_async_copy(u, u, a1_send).wait()
    rest = pl_in.at[pl.ds(0, 31)]
    pltpu.make_async_copy(rest, rest, a2_send).wait()
    rest = rl.at[pl.ds(0, 31)]
    pltpu.make_async_copy(rest, rest, r_send).wait()


def finish(parts, out):
    total = jnp.sum(parts[...], axis=0)
    for s in range(9):
        out[s] = total[s // 8:s // 8 + 1, 16 * (s % 8):16 * (s % 8) + 16]


def body(fitting_vectors):
    ly, lyi, bz, bzi, kt, trig = constants()
    rows = fitting_vectors.reshape(16, 2, 8, 128).transpose(0, 2, 1, 3).reshape(16, 16, 128)
    any_spec = pl.BlockSpec(memory_space=pl.ANY)
    dma = pltpu.SemaphoreType.DMA
    partial = pl.pallas_call(
        functools.partial(body_kernel, trig),
        name="coulomb",
        out_shape=jax.ShapeDtypeStruct((32, 2, 128), F32),
        in_specs=[any_spec] * 6,
        out_specs=any_spec,
        scratch_shapes=[
            pltpu.VMEM((256, 128), F32),
            pltpu.VMEM((256, 128), F32),
            pltpu.VMEM((32, 8, 128), F32),
            pltpu.VMEM((160, 8, 128), F32),
            pltpu.VMEM((32, 8, 128), F32),
            pltpu.VMEM(ly.shape, BF16),
            pltpu.VMEM(lyi.shape, BF16),
            pltpu.VMEM(bz.shape, BF16),
            pltpu.VMEM(bzi.shape, BF16),
            pltpu.VMEM(kt.shape, F32),
            pltpu.VMEM((96, 2048), BF16),
            pltpu.VMEM((512, 256), BF16),
            pltpu.VMEM((512, 256), BF16),
            pltpu.VMEM((512, 512), BF16),
            pltpu.VMEM((512, 512), BF16),
            pltpu.VMEM((192, 2048), BF16),
            pltpu.VMEM((32, 2048), F32),
            pltpu.VMEM((160, 1024), BF16),
            pltpu.VMEM((160, 1024), BF16),
            pltpu.VMEM((32, 2, 128), F32),
            pltpu.SemaphoreType.REGULAR,
            pltpu.SemaphoreType.REGULAR,
            dma((5,)),
            dma, dma,
            dma((14 * PIECES,)), dma((12 * PIECES,)), dma,
            dma, dma, dma,
            dma, dma, dma,
        ],
        compiler_params=pltpu.CompilerParams(collective_id=0, has_side_effects=True),
    )(rows, ly, lyi, bz, bzi, kt)
    out = pl.pallas_call(
        finish,
        name="finish",
        out_shape=jax.ShapeDtypeStruct((9, 1, 16), F32),
        in_specs=[pl.BlockSpec(memory_space=pltpu.VMEM)],
        out_specs=pl.BlockSpec(memory_space=pltpu.VMEM),
    )(partial)
    return out.transpose(1, 0, 2)


def solution(mesh):
    return jax.shard_map(
        body,
        mesh=mesh,
        in_specs=(P("vec", "grid", None),),
        out_specs=P(("vec", "grid"), None, None),
        check_vma=False,
    )
```
